128 devices in a mesh: lat: 32 (over z, y, core), lev: 4 (over x).
Axes of the slice: x: 4, y: 4, z: 4, core: 2. Of those that a mesh axis runs over, the one named last changes fastest.
Arguments:
- grid: bfloat16 [3, 1536, 32, 2816], P(None, 'lat', 'lev'), may hold values from -6 to 6
- legendre: bfloat16 [384, 769, 1280], P(('lat', 'lev')), may hold values from -6 to 6
- gauss_weights: float32 [1280], replicated, may hold values from 0.00078125 to 0.003125
- band_counts: int32 [32], replicated, may hold values from 1 to 48, 1280 in all
- pair_m: int32 [384], replicated, may hold values from 0 to 383, each once
- vert_modes: float32 [32, 32], replicated, may hold values from -1 to 1
- mode_depth: float32 [32], replicated, may hold values from 0.5 to 50
- diffusion: float32 [32], replicated, may hold values from 1 to 100
- pressure_balance_matrix: float32 [32, 32], replicated, may hold values from -1 to 1
Outputs:
- next_grid_rows: bfloat16 [3, 1536, 32, 2816], P(None, 'lat', 'lev')
The draws below stay inside these ranges and needn't reach their ends.
Inputs may be any that keep to these rules, and one draw needn't show every extreme that they name: `band_counts`: latitudes in each band, in band order; the bands cover all 1280 latitudes and the fullest holds 48. `pair_m`: each of 0 to 383 once.
All inputs are finite; a program needn't handle non-finite values.
Results may differ from the reference program's by a relative error of at most 0.0072.
Values may be sent and summed in bfloat16 or wider, within the bound.
A program may use at most 256 MiB of HBM per device.

```python
import math
import jax
import jax.numpy as jnp
import numpy as np
from jax import lax

M = 768
NLAT = 1280
NLON = 2816
LEVELS = 32
BAND_ROW_LIMIT = 48
SLOTS = 1536
PAIRS = 384
N_LAT = 32


def shard_levels(stream_key, shape, cuts, low, largest):
    def one(dim, blocks):
        steps = jax.random.uniform(jax.random.fold_in(jax.random.fold_in(stream_key, 6), dim), (blocks,), jnp.float32, low / len(cuts), largest / len(cuts))
        return jnp.repeat(jnp.exp(steps), shape[dim] // blocks).reshape((-1,) + (1,) * (len(shape) - dim - 1))

    gain = one(*cuts[0])
    for cut in cuts[1:]:
        gain = gain * one(*cut)
    return gain


def length_profile(number_of, total, most, skew):
    portions = [(1 << 20) // math.isqrt(grade ** skew) + 1 for grade in range(2, number_of + 1)]
    rest, given = total - most - (number_of - 1), [1] * (number_of - 1)
    while rest > 0:
        movable = [i for i in range(number_of - 1) if given[i] < most]
        mass, budget = sum([portions[i] for i in movable]), rest
        for i in movable:
            more = min(most - given[i], max(1, budget * portions[i] // mass), rest)
            given[i] = given[i] + more
            rest = rest - more
    return np.array([most] + given)


def uneven(stream_key, amount, total, reach, skew):
    if amount == 2:
        one = jax.random.randint(stream_key, (), max(1, total - reach), min(reach, total - 1) + 1)
        return jnp.stack([one, total - one])
    sizes = jnp.asarray(length_profile(amount, total, reach, skew), jnp.int32)
    twos = (amount - 1) // 2
    giver, taker = sizes[1:1 + 2 * twos:2], sizes[2:2 + 2 * twos:2]
    room = jnp.minimum(giver - 1, reach - taker)
    passed = jax.random.randint(jax.random.fold_in(stream_key, 1), (twos,), 0, 1 << 20) % (room + 1)
    sizes = sizes.at[1:1 + 2 * twos:2].set(giver - passed).at[2:2 + 2 * twos:2].set(taker + passed)
    return sizes[jax.random.permutation(jax.random.fold_in(stream_key, 2), amount)]


def noise(stream_key, extent, spread, reach, cuts=(), held_as=jnp.bfloat16):
    values = spread * jax.random.normal(stream_key, extent, jnp.float32)
    if cuts:
        values = values * shard_levels(stream_key, extent, cuts, -0.22, 0.18)
    return jnp.clip(values, -reach, reach).astype(held_as)


def setup_inputs(seed: int = 0) -> dict:
    streams_of = jax.random.split(jax.random.key(seed), 10)
    grid = noise(streams_of[0], (3, SLOTS, LEVELS, NLON), 1.0, 6.0, ((1, 32), (2, 4)))
    legendre = noise(streams_of[1], (PAIRS, M + 1, NLAT), 1.0, 6.0, ((0, 128),))
    gauss_weights = jnp.clip(jnp.exp(jax.random.uniform(streams_of[2], (NLAT,), jnp.float32, math.log(0.00078125), math.log(0.003125))), 0.00078125, 0.003125)
    band_counts = uneven(streams_of[3], N_LAT, NLAT, BAND_ROW_LIMIT, 1).astype(jnp.int32)
    pair_m = jax.random.permutation(streams_of[4], PAIRS).astype(jnp.int32)
    vert_modes = noise(streams_of[5], (LEVELS, LEVELS), LEVELS ** -0.5, 1.0, (), jnp.float32)
    mode_depth = jnp.clip(jnp.exp(jax.random.uniform(streams_of[6], (LEVELS,), jnp.float32, math.log(0.5), math.log(50.0))), 0.5, 50.0)
    diffusion = jnp.clip(jnp.exp(jax.random.uniform(streams_of[7], (LEVELS,), jnp.float32, math.log(1.0), math.log(100.0))), 1.0, 100.0)
    pressure_balance_matrix = noise(streams_of[8], (LEVELS, LEVELS), LEVELS ** -0.5, 1.0, (), jnp.float32)
    return {"grid": grid, "legendre": legendre, "gauss_weights": gauss_weights, "band_counts": band_counts, "pair_m": pair_m, "vert_modes": vert_modes, "mode_depth": mode_depth, "diffusion": diffusion, "pressure_balance_matrix": pressure_balance_matrix}


def dft_tables(pair_m, width, points):
    lower_wave = pair_m.astype(jnp.int32)
    upper_wave = (width - 1 - lower_wave).astype(jnp.int32)
    harmonic_order_index = jnp.stack([lower_wave, lower_wave, upper_wave, upper_wave], axis=1).reshape(-1)
    component = jnp.arange(2 * width, dtype=jnp.int32) % 2
    phase_index = (harmonic_order_index[:, None] * jnp.arange(points, dtype=jnp.int32)[None, :]) % points
    angles = phase_index.astype(jnp.float32) * (2.0 * math.pi / points)
    trig_values = jnp.where((component == 0)[:, None], jnp.cos(angles), -jnp.sin(angles))
    factor = jnp.where(harmonic_order_index == 0, 1.0, 2.0).astype(jnp.float32)
    forward_table = (trig_values / points).astype(jnp.bfloat16)
    inverse_table = (trig_values * factor[:, None]).astype(jnp.bfloat16)
    return forward_table, inverse_table


def latitude_maps(band_counts, lat_cap, lat_total):
    counts = band_counts.astype(jnp.int32)
    group_count = counts.shape[0]
    band_starts = (jnp.cumsum(counts) - counts).astype(jnp.int32)
    groups = jnp.arange(group_count, dtype=jnp.int32)
    latitude_list = jnp.arange(lat_total, dtype=jnp.int32)
    lat_band = jnp.sum((band_starts[None, :] <= latitude_list[:, None]).astype(jnp.int32), axis=1).astype(jnp.int32) - 1
    lat_begin = jnp.sum(jnp.where(groups[None, :] == lat_band[:, None], band_starts[None, :], 0), axis=1).astype(jnp.int32)
    slot_for_latitude = (lat_band * lat_cap + latitude_list - lat_begin).astype(jnp.int32)
    slot_ids = jnp.arange(group_count * lat_cap, dtype=jnp.int32)
    slot_band = slot_ids // lat_cap
    offsets = slot_ids % lat_cap
    member = groups[None, :] == slot_band[:, None]
    slot_begin = jnp.sum(jnp.where(member, band_starts[None, :], 0), axis=1).astype(jnp.int32)
    slot_size = jnp.sum(jnp.where(member, counts[None, :], 0), axis=1).astype(jnp.int32)
    valid_slot = offsets < slot_size
    lat_of_slot = jnp.where(valid_slot, slot_begin + offsets, 0).astype(jnp.int32)
    return slot_for_latitude, lat_of_slot, valid_slot


def helmholtz(harmonic_model_snapshot, ratio, vert_modes, mode_depth, diffusion, pressure_balance_matrix):
    rotation_harmonic_coeffs = harmonic_model_snapshot[..., 0, :, :]
    velocity_spread_coeffs_map = harmonic_model_snapshot[..., 1, :, :]
    thermal_harmonic_coeffs = harmonic_model_snapshot[..., 2, :, :]
    rotation_harmonic_coeffs = rotation_harmonic_coeffs / (1.0 + diffusion[:, None] * ratio * ratio)
    modes = jnp.einsum('ql,...lk->...qk', vert_modes, velocity_spread_coeffs_map, precision=lax.Precision.HIGHEST)
    modes = modes / (1.0 + mode_depth[:, None] * ratio)
    velocity_spread_coeffs_map = jnp.einsum('ql,...qk->...lk', vert_modes, modes, precision=lax.Precision.HIGHEST)
    thermal_harmonic_coeffs = thermal_harmonic_coeffs - jnp.einsum('ja,...ax->...jx', pressure_balance_matrix, velocity_spread_coeffs_map, precision=lax.Precision.HIGHEST)
    return jnp.stack([rotation_harmonic_coeffs, velocity_spread_coeffs_map, thermal_harmonic_coeffs], axis=-3)


def reference(grid, legendre, gauss_weights, band_counts, pair_m, vert_modes, mode_depth, diffusion, pressure_balance_matrix):
    slot_for_latitude, lat_of_slot, valid_slot = latitude_maps(band_counts, BAND_ROW_LIMIT, NLAT)
    forward_table, inverse_table = dft_tables(pair_m, M, NLON)
    slot_weights = jnp.where(valid_slot, gauss_weights[lat_of_slot], 0.0).astype(jnp.float32)

    def analyse(field_grid):
        flat_grid = field_grid.reshape(SLOTS * LEVELS, NLON)
        coeffs = jnp.dot(forward_table, flat_grid.T, preferred_element_type=jnp.float32)
        return (coeffs.reshape(2 * M, SLOTS, LEVELS) * slot_weights[None, :, None]).astype(jnp.bfloat16)

    fourier = lax.map(analyse, grid)
    ordered = jnp.take(fourier, slot_for_latitude, axis=2)
    ordered = ordered.reshape(3, PAIRS, 2, 2, NLAT, LEVELS).transpose(1, 2, 3, 0, 5, 4)
    ordered = ordered.reshape(PAIRS, 2, 2, 3 * LEVELS, NLAT)
    half_rows = M // 2 + 1

    def each_mode_couple(inputs):
        table, coeffs, wave = inputs
        table_full = table.astype(jnp.float32)
        table_head = table_full[:half_rows]
        table_tail = table_full[half_rows:]
        coeffs_full = coeffs.astype(jnp.float32)
        row_ids = jnp.arange(M + 1, dtype=jnp.int32)
        own_rows = row_ids < M - wave
        degree = jnp.where(own_rows, wave + row_ids, row_ids - 1)
        ratio = (degree * (degree + 1)).astype(jnp.float32) / float(M * (M - 1))
        head_spec = jnp.einsum('kj,rcj->rck', table_head, coeffs_full[0])
        tail_both = jnp.einsum('kj,wrcj->wrck', table_tail, coeffs_full)
        tail_own = own_rows[half_rows:]
        tail_spec = jnp.where(tail_own, tail_both[0], tail_both[1])
        harmonic_model_snapshot = jnp.concatenate([head_spec, tail_spec], axis=-1).reshape(2, 3, LEVELS, M + 1)
        updated = helmholtz(harmonic_model_snapshot, ratio, vert_modes, mode_depth, diffusion, pressure_balance_matrix).astype(jnp.bfloat16)
        updated = updated.reshape(2, 3 * LEVELS, M + 1).astype(jnp.float32)
        head_part = jnp.einsum('kj,rck->rcj', table_head, updated[..., :half_rows])
        masks = jnp.stack([tail_own, jnp.logical_not(tail_own)]).astype(jnp.float32)
        masked = updated[None, :, :, half_rows:] * masks[:, None, None, :]
        tail_parts = jnp.einsum('kj,wrck->wrcj', table_tail, masked)
        synthesis = jnp.stack([tail_parts[0] + head_part, tail_parts[1]])
        return synthesis.astype(jnp.bfloat16)

    gridpoint = lax.map(each_mode_couple, (legendre, ordered, pair_m.astype(jnp.int32)))
    banded = jnp.take(gridpoint, lat_of_slot, axis=4) * valid_slot.astype(jnp.bfloat16)
    banded = jnp.moveaxis(banded.reshape(2 * M, 3, LEVELS * SLOTS), 1, 0)

    def synthesise(field_coeffs):
        values = jnp.dot(field_coeffs.T, inverse_table, preferred_element_type=jnp.float32)
        return values.reshape(LEVELS, SLOTS, NLON).transpose(1, 0, 2).astype(jnp.bfloat16)

    return lax.map(synthesise, banded)
```

```python
import math

import jax
import jax.numpy as jnp
from jax import lax
from jax.experimental import pallas as pl
from jax.experimental.pallas import tpu as pltpu
from jax.sharding import PartitionSpec as P


def dft_tables(pair_m, width, points):
    upper_wave = width - 1 - pair_m
    harmonic_order_index = jnp.stack([pair_m, pair_m, upper_wave, upper_wave], axis=1).reshape(-1)
    component = jnp.arange(2 * width, dtype=jnp.int32) % 2
    phase_index = (
        harmonic_order_index[:, None] * jnp.arange(points, dtype=jnp.int32)[None, :] % points
    )
    angles = phase_index.astype(jnp.float32) * (2.0 * math.pi / points)
    trig_values = jnp.where((component == 0)[:, None], jnp.cos(angles), -jnp.sin(angles))
    factor = jnp.where(harmonic_order_index == 0, 1.0, 2.0).astype(jnp.float32)
    forward_table = (trig_values / points).astype(jnp.bfloat16)
    inverse_table = (trig_values * factor[:, None]).astype(jnp.bfloat16)
    return (forward_table, inverse_table)


def latitude_maps(band_counts, lat_cap):
    group_count = band_counts.shape[0]
    band_starts = jnp.cumsum(band_counts) - band_counts
    groups = jnp.arange(group_count, dtype=jnp.int32)
    slot_ids = jnp.arange(group_count * lat_cap, dtype=jnp.int32)
    slot_band = slot_ids // lat_cap
    offsets = slot_ids % lat_cap
    member = groups[None, :] == slot_band[:, None]
    slot_begin = jnp.sum(jnp.where(member, band_starts[None, :], 0), axis=1)
    slot_size = jnp.sum(jnp.where(member, band_counts[None, :], 0), axis=1)
    valid_slot = offsets < slot_size
    lat_of_slot = jnp.where(valid_slot, slot_begin + offsets, 0)
    return (lat_of_slot, valid_slot, band_starts)


def helmholtz(
    harmonic_model_snapshot, ratio, vert_modes, mode_depth, diffusion, pressure_balance_matrix
):
    rotation_harmonic_coeffs = harmonic_model_snapshot[..., 0, :, :]
    velocity_spread_coeffs_map = harmonic_model_snapshot[..., 1, :, :]
    thermal_harmonic_coeffs = harmonic_model_snapshot[..., 2, :, :]
    rotation_harmonic_coeffs = rotation_harmonic_coeffs / (1.0 + diffusion[:, None] * ratio * ratio)
    modes = jnp.einsum(
        "ql,...lk->...qk", vert_modes, velocity_spread_coeffs_map, precision=lax.Precision.HIGHEST
    )
    modes = modes / (1.0 + mode_depth[:, None] * ratio)
    velocity_spread_coeffs_map = jnp.einsum(
        "ql,...qk->...lk", vert_modes, modes, precision=lax.Precision.HIGHEST
    )
    thermal_harmonic_coeffs = thermal_harmonic_coeffs - jnp.einsum(
        "ja,...ax->...jx",
        pressure_balance_matrix,
        velocity_spread_coeffs_map,
        precision=lax.Precision.HIGHEST,
    )
    return jnp.stack(
        [rotation_harmonic_coeffs, velocity_spread_coeffs_map, thermal_harmonic_coeffs], axis=-3
    )


def exchange_kernel(x, o, send, recv, local):
    lat, lev = lax.axis_index("lat"), lax.axis_index("lev")
    me = lat * 4 + lev
    barrier = pltpu.get_barrier_semaphore()

    def greet(k, carry):
        there = lax.rem(me + k, 128)
        pl.semaphore_signal(
            barrier,
            inc=1,
            device_id=(there // 4, lax.rem(there, 4)),
            device_id_type=pl.DeviceIdType.MESH,
        )
        return carry

    lax.fori_loop(1, 128, greet, 0)
    pl.semaphore_wait(barrier, 127)
    own = pltpu.make_async_copy(x.at[me], o.at[me], local)
    own.start()

    def launch(k, carry):
        step = lax.rem(k * 37, 128)
        z = lax.rem(lat // 8 + step // 32, 4)
        y = lax.rem(lat // 2 + step // 8, 4)
        core = lax.rem(lat + step, 2)
        to_lat, to_lev = (z * 4 + y) * 2 + core, lax.rem(lev + step // 2, 4)
        pltpu.make_async_remote_copy(
            src_ref=x.at[to_lat * 4 + to_lev],
            dst_ref=o.at[me],
            send_sem=send,
            recv_sem=recv,
            device_id=(to_lat, to_lev),
            device_id_type=pl.DeviceIdType.MESH,
        ).start()
        return carry

    lax.fori_loop(1, 128, launch, 0)
    own.wait()
    rest = pltpu.make_async_remote_copy(
        src_ref=x.at[pl.ds(0, 127)],
        dst_ref=o.at[pl.ds(0, 127)],
        send_sem=send,
        recv_sem=recv,
        device_id=(lat, lev),
        device_id_type=pl.DeviceIdType.MESH,
    )
    rest.wait_send()
    rest.wait_recv()


def exchange(x, number):
    shape = x.shape
    x = x.reshape(shape[0], -1, 128)
    return pl.pallas_call(
        exchange_kernel,
        out_shape=jax.ShapeDtypeStruct(x.shape, x.dtype),
        in_specs=[pl.BlockSpec(memory_space=pl.ANY)],
        out_specs=pl.BlockSpec(memory_space=pl.ANY),
        scratch_shapes=[pltpu.SemaphoreType.DMA] * 3,
        compiler_params=pltpu.CompilerParams(collective_id=number, has_side_effects=True),
    )(x).reshape(shape)


def shards(
    grid,
    legendre,
    gauss_weights,
    band_counts,
    pair_m,
    vert_modes,
    mode_depth,
    diffusion,
    pressure_balance_matrix,
):
    lat_groups = lax.axis_size("lat")
    lev_groups = lax.axis_size("lev")
    device_count = lat_groups * lev_groups
    fields, lat_cap, lev_dev, points = grid.shape
    pair_dev, row_count, lat_total = legendre.shape
    width = row_count - 1
    half_rows = width // 2 + 1
    level_total = lev_dev * lev_groups
    my_band = lax.axis_index("lat")
    owner_index = my_band * lev_groups + lax.axis_index("lev")
    lat_of_slot, valid_slot, band_starts = latitude_maps(band_counts, lat_cap)
    band_match = jnp.arange(lat_groups, dtype=jnp.int32) == my_band
    my_start = jnp.sum(jnp.where(band_match, band_starts, 0))
    my_count = jnp.sum(jnp.where(band_match, band_counts, 0))
    row_valid = jnp.arange(lat_cap, dtype=jnp.int32) < my_count
    padded_weights = jnp.concatenate([gauss_weights, jnp.zeros((lat_cap,), jnp.float32)])
    row_weights = jnp.where(
        row_valid, lax.dynamic_slice(padded_weights, (my_start,), (lat_cap,)), 0.0
    )
    forward_table, inverse_table = dft_tables(pair_m, width, points)
    coeffs = lax.dot_general(
        forward_table, grid, (((1,), (3,)), ((), ())), preferred_element_type=jnp.float32
    )
    coeffs = (coeffs * row_weights[None, None, :, None]).astype(jnp.bfloat16)
    coeffs = coeffs.reshape(device_count, pair_dev * 4, fields, lat_cap * lev_dev)
    slot_table = jnp.take(legendre, lat_of_slot, axis=2) * valid_slot.astype(jnp.bfloat16)
    slot_table = slot_table.reshape(pair_dev, row_count, lat_groups, lat_cap)
    table_head = slot_table[:, :half_rows]
    table_tail = slot_table[:, half_rows:]
    local_waves = lax.dynamic_slice(pair_m, (owner_index * pair_dev,), (pair_dev,))
    row_ids = jnp.arange(row_count, dtype=jnp.int32)
    own_rows = row_ids[None, :] < (width - local_waves)[:, None]
    degree = jnp.where(own_rows, local_waves[:, None] + row_ids[None, :], row_ids[None, :] - 1)
    ratio = (degree * (degree + 1)).astype(jnp.float32) / float(width * (width - 1))
    tail_own = own_rows[:, half_rows:]
    received = exchange(coeffs, 0)
    field_part = received.shape[2]
    arranged = received.reshape(
        lat_groups, lev_groups, pair_dev, 2, 2, field_part, lat_cap, lev_dev
    )
    head_spec = jnp.einsum(
        "pkgs,glpcfsd->pcfldk", table_head, arranged[:, :, :, 0], preferred_element_type=jnp.float32
    )
    tail_both = jnp.einsum(
        "pkgs,glpwcfsd->pwcfldk", table_tail, arranged, preferred_element_type=jnp.float32
    )
    tail_spec = jnp.where(tail_own[:, None, None, None, None, :], tail_both[:, 0], tail_both[:, 1])
    harmonic_model_snapshot = jnp.concatenate([head_spec, tail_spec], axis=-1)
    harmonic_space_module = harmonic_model_snapshot.reshape(
        pair_dev, 2, field_part, level_total, row_count
    )
    updated = helmholtz(
        harmonic_space_module,
        ratio[:, None, None, :],
        vert_modes,
        mode_depth,
        diffusion,
        pressure_balance_matrix,
    ).astype(jnp.bfloat16)
    updated = updated.reshape(pair_dev, 2, fields, lev_groups, lev_dev, row_count)
    head_part = jnp.einsum(
        "pkgs,prfldk->glprfsd",
        table_head,
        updated[..., :half_rows],
        preferred_element_type=jnp.float32,
    )
    masks = jnp.stack([tail_own, jnp.logical_not(tail_own)], axis=1).astype(jnp.bfloat16)
    masked = updated[:, None, ..., half_rows:] * masks[:, :, None, None, None, None, :]
    tail_parts = jnp.einsum(
        "pkgs,pwrfldk->glpwrfsd", table_tail, masked, preferred_element_type=jnp.float32
    )
    synthesis = jnp.stack(
        [tail_parts[:, :, :, 0] + head_part, tail_parts[:, :, :, 1]], axis=3
    ).astype(jnp.bfloat16)
    banded = synthesis.reshape(device_count, pair_dev * 4, fields, lat_cap * lev_dev)
    received = exchange(banded, 1)
    field_part = received.shape[2]
    columns = received.reshape(2 * width, field_part, lat_cap * lev_dev)
    values = lax.dot_general(
        columns, inverse_table, (((0,), (0,)), ((), ())), preferred_element_type=jnp.float32
    )
    return values.reshape(field_part, lat_cap, lev_dev, points).astype(jnp.bfloat16)


def solution(mesh):
    placed = (
        P(None, "lat", "lev", None),
        P(("lat", "lev"), None, None),
        P(),
        P(),
        P(),
        P(),
        P(),
        P(),
        P(),
    )
    return jax.shard_map(
        shards, mesh=mesh, in_specs=placed, out_specs=P(None, "lat", "lev", None), check_vma=False
    )
```

```python
import functools
import math

import jax
import jax.numpy as jnp
from jax import lax
from jax.experimental import pallas as pl
from jax.experimental.pallas import tpu as pltpu
from jax.sharding import PartitionSpec as P

WIDTH = 768
NLAT = 1280
POINTS = 2816
ROWS = 784
DEPTH = 896
BANDS = 32
F32, BF16 = jnp.float32, jnp.bfloat16

WINDOWS = ((0, 384), (128, 640), (512, 640), (896, 384))


def swap(a, b, bit, low):
    return (
        jnp.where(low, a, pltpu.roll(b, bit, 1)),
        jnp.where(low, pltpu.roll(a, 128 - bit, 1), b),
    )


def exchange_bits(arrays, base, lane):
    arrays = list(arrays)
    step = 1
    while step < len(arrays):
        bit = base * step
        low = (lane & bit) == 0
        for i in range(len(arrays)):
            if not i & step:
                arrays[i], arrays[i | step] = swap(arrays[i], arrays[i | step], bit, low)
        step *= 2
    return arrays


def lanes_of(rows=16):
    return lax.broadcasted_iota(jnp.int32, (rows, 128), 1)


def cos_sin(value, turn):
    quarter = POINTS // 4
    index = jnp.floor(value * (1.0 / quarter) + 0.5)
    angle = (value - index * quarter) * (2.0 * math.pi / POINTS)
    sq = angle * angle
    c = 1.0 + sq * (-0.5 + sq * (1 / 24 + sq * (-1 / 720 + sq * (1 / 40320))))
    s = angle * (1.0 + sq * (-1 / 6 + sq * (1 / 120 + sq * (-1 / 5040))))
    index = (index.astype(jnp.int32) + turn) & 3
    odd = (index & 1) == 1
    cos = jnp.where(odd, s, c)
    sin = jnp.where(odd, c, s)
    cos = jnp.where((index == 1) | (index == 2), -cos, cos)
    sin = jnp.where(index >= 2, -sin, sin)
    return cos, sin


def make_table(p, wave, part, table, b_cos, b_sin, a_cos, a_sin):
    w = wave[p]
    row = lax.broadcasted_iota(jnp.int32, (128, 512), 0).astype(F32)
    b_cos[...], b_sin[...] = cos_sin(row * w, 0)
    row = lax.broadcasted_iota(jnp.int32, (24, 512), 0).astype(F32)
    a_cos[...], a_sin[...] = cos_sin(row * (128.0 * w), part[p])

    def fill(a, carry):
        values = a_cos[pl.ds(a, 1), :] * b_cos[...] - a_sin[pl.ds(a, 1), :] * b_sin[...]
        table[p, pl.ds(pl.multiple_of(a * 128, 128), 128), :] = values.astype(BF16)
        return carry

    lax.fori_loop(0, POINTS // 128, fill, 0)


def analyse(p, grid, weight, table, y, chunks):
    lane = lanes_of()

    def field(f, carry):
        base = pl.multiple_of(f * 384, 384)
        values = jnp.dot(grid[pl.ds(base, 384), :], table[p], preferred_element_type=F32)
        for tile in range(4):
            y[tile] = values[:, tile * 128 : tile * 128 + 128] * weight[...]

        def chunk(n, carry):
            third, tile = n // 4, lax.rem(n, 4)
            levels = [y[tile, pl.ds(third * 128 + l, 16, stride=8), :] for l in range(8)]
            for e, out in enumerate(exchange_bits(levels, 1, lane)):
                chunks[9 * p + 3 * f + third, tile * 8 + e] = out.astype(BF16)
            return carry

        return lax.fori_loop(0, 12, chunk, carry)

    lax.fori_loop(0, 3, field, 0)


def pack_chunks(t, chunks, send):
    lane = lanes_of()

    def group(i, carry):
        parts = [chunks[4 * t + g, i].astype(F32) for g in range(4)]
        for x, out in enumerate(exchange_bits(parts, 32, lane)):
            send[4 * i + x, t] = out.astype(BF16)
        return carry

    lax.fori_loop(0, BANDS, group, 0)


def forward_kernel(grid, wave, part, weight, send, table, b_cos, b_sin, a_cos, a_sin, y, chunks):
    chunks[27] = jnp.zeros(chunks.shape[1:], BF16)
    for p in range(3):
        make_table(p, wave, part, table, b_cos, b_sin, a_cos, a_sin)
        analyse(p, grid, weight, table, y, chunks)
        for t in range(2 * p, 2 * p + (3 if p == 2 else 2)):
            pack_chunks(t, chunks, send)


def spread_legendre(p, legendre, slot_row, slot_column, wide, tall):
    wide[p, 768:ROWS, :] = jnp.zeros((16, 1536), BF16)
    tall[p, :, 768:DEPTH] = jnp.zeros((1536, 128), BF16)
    for tile, (low, size) in enumerate(WINDOWS):
        at = tile * 384
        part = legendre[p, :, low : low + size]
        row = lax.broadcasted_iota(jnp.int32, (size, 384), 0) + low
        pick = jnp.where(row == slot_row[:, at : at + 384], 1.0, 0.0).astype(BF16)
        wide[p, 0 : WIDTH + 1, at : at + 384] = jnp.dot(
            part, pick, preferred_element_type=F32
        ).astype(BF16)
        row = lax.broadcasted_iota(jnp.int32, (384, size), 1) + low
        pick = jnp.where(row == slot_column[at : at + 384, :], 1.0, 0.0).astype(BF16)
        tall[p, at : at + 384, 0 : WIDTH + 1] = lax.dot_general(
            pick, part, (((1,), (1,)), ((), ())), preferred_element_type=F32
        ).astype(BF16)


def gather_tiles(t, received, fourier):
    lane = lanes_of()

    def band(b, carry):
        parts = [received[4 * b + v, t].astype(F32) for v in range(4)]
        for g, out in enumerate(exchange_bits(parts, 32, lane)):
            q = 4 * t + g
            if q < 27:
                f, third = q % 9 // 3, q % 3
                row = pl.multiple_of(b * 48 + third * 16, 16)
                fourier[q // 9, pl.ds(row, 16), f * 128 : f * 128 + 128] = out.astype(BF16)
        return carry

    lax.fori_loop(0, BANDS, band, 0)


def spectral_step(p, own_wave, lane_scales, mixes, wide, tall, fourier, spectral, updated, synthesis):
    wave = own_wave[p]
    spectral[...] = jnp.dot(wide[p], fourier[p], preferred_element_type=F32)
    exact = functools.partial(
        jnp.dot, precision=lax.Precision.HIGHEST, preferred_element_type=F32
    )
    upper = (lanes_of(112) & 16) != 0
    updated[ROWS:DEPTH, :] = jnp.zeros((DEPTH - ROWS, 384), BF16)

    def block(i, carry):
        at = pl.multiple_of(i * 112, 112)
        k = lax.broadcasted_iota(jnp.int32, (112, 128), 0) + at
        own = k < WIDTH - wave
        degree = jnp.where(own, wave + k, k - 1)
        ratio = (degree * (degree + 1)).astype(F32) / float(WIDTH * (WIDTH - 1))
        keep = (own != upper) & (k <= WIDTH)
        rows = pl.ds(at, 112)
        first = spectral[rows, 0:128] / (1.0 + lane_scales[0:1, :] * ratio * ratio)
        modes = exact(spectral[rows, 128:256], mixes[0])
        modes = modes / (1.0 + lane_scales[1:2, :] * ratio)
        second = exact(modes, mixes[1])
        third = spectral[rows, 256:384] - exact(second, mixes[2])
        for f, values in enumerate((first, second, third)):
            updated[rows, f * 128 : f * 128 + 128] = jnp.where(keep, values, 0.0).astype(BF16)
        return carry

    lax.fori_loop(0, ROWS // 112, block, 0)
    double = (lax.broadcasted_iota(jnp.int32, (1, 384), 1) & 16 != 0) | (wave > 0)
    factor = jnp.where(double, 2.0, 1.0)

    def rows_of(i, carry):
        at = pl.multiple_of(i * 384, 384)
        values = jnp.dot(tall[p, pl.ds(at, 384), :], updated[...], preferred_element_type=F32)
        synthesis[p, pl.ds(at, 384), :] = (values * factor).astype(BF16)
        return carry

    lax.fori_loop(0, 4, rows_of, 0)


def scatter_tiles(t, synthesis, send):
    lane = lanes_of()

    def band(b, carry):
        parts = []
        for g in range(4):
            q = min(4 * t + g, 26)
            f, third = q % 9 // 3, q % 3
            row = pl.multiple_of(b * 48 + third * 16, 16)
            parts.append(
                synthesis[q // 9, pl.ds(row, 16), f * 128 : f * 128 + 128].astype(F32)
            )
        for v, out in enumerate(exchange_bits(parts, 32, lane)):
            send[4 * b + v, t] = out.astype(BF16)
        return carry

    lax.fori_loop(0, BANDS, band, 0)


def middle_kernel(
    received, legendre, slot_row, slot_column, own_wave, lane_scales, mixes,
    send, wide, tall, fourier, spectral, updated, synthesis,
):
    for p in range(3):
        spread_legendre(p, legendre, slot_row, slot_column, wide, tall)
    for t in range(7):
        gather_tiles(t, received, fourier)
    for p in range(3):
        spectral_step(
            p, own_wave, lane_scales, mixes, wide, tall, fourier, spectral, updated, synthesis
        )
    for t in range(7):
        scatter_tiles(t, synthesis, send)


def open_tiles(t, received, chunks):
    lane = lanes_of()

    def group(i, carry):
        parts = [received[4 * i + x, t].astype(F32) for x in range(4)]
        for g, out in enumerate(exchange_bits(parts, 32, lane)):
            if 4 * t + g < 27:
                chunks[4 * t + g, i] = out.astype(BF16)
        return carry

    lax.fori_loop(0, BANDS, group, 0)


def synthesise(f, chunks, table, y, columns, out):
    lane = lanes_of()

    def chunk(n, carry):
        tile, third = n // 3, lax.rem(n, 3)
        p, eighth = tile // 4, lax.rem(tile, 4)
        parts = [chunks[9 * p + 3 * f + third, eighth * 8 + e].astype(F32) for e in range(8)]
        for l, values in enumerate(exchange_bits(parts, 1, lane)):
            y[tile, pl.ds(third * 128 + l, 16, stride=8), :] = values
        return carry

    lax.fori_loop(0, 36, chunk, 0)
    for tile in range(12):
        columns[:, tile * 128 : tile * 128 + 128] = y[tile].astype(BF16)
    base = pl.multiple_of(f * 384, 384)

    def points(i, carry):
        at = pl.multiple_of(i * 256, 256)
        total = jnp.zeros((384, 256), F32)
        for p in range(3):
            total = total + lax.dot_general(
                columns[:, p * 512 : p * 512 + 512],
                table[p, pl.ds(at, 256), :],
                (((1,), (1,)), ((), ())),
                preferred_element_type=F32,
            )
        out[pl.ds(base, 384), pl.ds(at, 256)] = total.astype(BF16)
        return carry

    lax.fori_loop(0, POINTS // 256, points, 0)


def inverse_kernel(received, table, out, y, columns, chunks):
    for t in range(7):
        open_tiles(t, received, chunks)

    def field(f, carry):
        synthesise(f, chunks, table, y, columns, out)
        return carry

    lax.fori_loop(0, 3, field, 0)


def call(kernel, inputs, spaces, outs, scratch, **params):
    vmem = pl.BlockSpec(memory_space=pltpu.VMEM)
    smem = pl.BlockSpec(memory_space=pltpu.SMEM)
    return pl.pallas_call(
        kernel,
        out_shape=[jax.ShapeDtypeStruct(s, d) for s, d in outs],
        in_specs=[smem if s == "s" else vmem for s in spaces],
        out_specs=[vmem] * len(outs),
        scratch_shapes=[pltpu.VMEM(s, d) for s, d in scratch],
        compiler_params=pltpu.CompilerParams(vmem_limit_bytes=62 * 2**20, **params),
    )(*inputs)


def shards(
    grid,
    legendre,
    gauss_weights,
    band_counts,
    pair_m,
    vert_modes,
    mode_depth,
    diffusion,
    pressure_balance_matrix,
):
    lev_groups = 4
    fields, lat_cap, lev_dev, points = grid.shape
    my_band = lax.axis_index("lat")
    owner = my_band * lev_groups + lax.axis_index("lev")
    band_starts = jnp.cumsum(band_counts) - band_counts
    offsets = jnp.arange(lat_cap, dtype=jnp.int32)
    slot = jnp.where(
        offsets[None, :] < band_counts[:, None], band_starts[:, None] + offsets[None, :], -1
    ).astype(jnp.int32)
    my_start = lax.dynamic_slice(band_starts, (my_band,), (1,))[0]
    my_count = lax.dynamic_slice(band_counts, (my_band,), (1,))[0]
    padded = jnp.concatenate([gauss_weights, jnp.zeros((lat_cap,), F32)])
    weight = lax.dynamic_slice(padded, (my_start,), (lat_cap,)) * (1.0 / POINTS)
    weight = jnp.where(offsets < my_count, weight, 0.0)
    weight = jnp.broadcast_to(weight[:, None, None], (lat_cap, lev_dev, 128)).reshape(384, 128)

    lower = pair_m.reshape(4, 8, 4, 3).transpose(3, 0, 2, 1)
    waves = jnp.stack([lower, WIDTH - 1 - lower], axis=3)
    waves = jnp.broadcast_to(waves[:, :, :, :, None, :], (3, 4, 4, 2, 2, 8))
    part = jnp.broadcast_to(
        jnp.arange(2, dtype=jnp.int32)[None, None, None, None, :, None], waves.shape
    ).reshape(3, 1, 512)
    waves = waves.reshape(3, 1, 512).astype(F32)
    own_wave = lax.dynamic_slice(pair_m, (owner * 3,), (3,))

    def over_lanes(v):
        v = v.reshape(4, 1, 8)
        return jnp.broadcast_to(v, (4, 4, 8)).reshape(128)

    def mix(m):
        m = m.reshape(4, 1, 8, 4, 1, 8) * jnp.eye(4, dtype=F32).reshape(1, 4, 1, 1, 4, 1)
        return m.reshape(128, 128)

    lane_scales = jnp.stack([over_lanes(diffusion), over_lanes(mode_depth)])
    mixes = jnp.stack([mix(vert_modes.T), mix(vert_modes), mix(pressure_balance_matrix.T)])

    block = (128, 7, 16, 128)
    small = [((128, 512), F32)] * 2 + [((24, 512), F32)] * 2
    send, table = call(
        forward_kernel,
        (grid.reshape(1152, points), waves, part, weight),
        "vvvv",
        [(block, BF16), ((3, points, 512), BF16)],
        small + [((4, 384, 128), F32), ((28, 32, 16, 128), BF16)],
    )
    received = lax.all_to_all(send, ("lat", "lev"), 0, 0, tiled=True)
    (send,) = call(
        middle_kernel,
        (received, legendre, slot.reshape(1, 1536), slot.reshape(1536, 1), own_wave, lane_scales, mixes),
        "vvvvsvv",
        [(block, BF16)],
        [
            ((3, ROWS, 1536), BF16),
            ((3, 1536, DEPTH), BF16),
            ((3, 1536, 384), BF16),
            ((ROWS, 384), F32),
            ((DEPTH, 384), BF16),
            ((3, 1536, 384), BF16),
        ],
    )
    received = lax.all_to_all(send, ("lat", "lev"), 0, 0, tiled=True)
    (out,) = call(
        inverse_kernel,
        (received, table),
        "vv",
        [((1152, points), BF16)],
        [((12, 384, 128), F32), ((384, 1536), BF16), ((28, 32, 16, 128), BF16)],
    )
    return out.reshape(fields, lat_cap, lev_dev, points)


def solution(mesh):
    placed = (
        P(None, "lat", "lev", None),
        P(("lat", "lev"), None, None),
        P(),
        P(),
        P(),
        P(),
        P(),
        P(),
        P(),
    )
    return jax.shard_map(
        shards, mesh=mesh, in_specs=placed, out_specs=P(None, "lat", "lev", None), check_vma=False
    )
```

```python
import math

import jax
import jax.numpy as jnp
from jax import lax
from jax.experimental import pallas as pl
from jax.experimental.pallas import tpu as pltpu
from jax.sharding import PartitionSpec as P

WIDTH = 768
NLAT = 1280
POINTS = 2816
ROWS = 784
DEPTH = 896
BANDS = 32
F32, BF16 = jnp.float32, jnp.bfloat16

WINDOWS = ((0, 384), (128, 640), (512, 640), (896, 384))


def swap(a, b, bit, low):
    return (
        jnp.where(low, a, pltpu.roll(b, bit, 1)),
        jnp.where(low, pltpu.roll(a, 128 - bit, 1), b),
    )


def exchange_bits(arrays, base, lane):
    arrays = list(arrays)
    step = 1
    while step < len(arrays):
        bit = base * step
        low = (lane & bit) == 0
        for i in range(len(arrays)):
            if not i & step:
                arrays[i], arrays[i | step] = swap(arrays[i], arrays[i | step], bit, low)
        step *= 2
    return arrays


def each(total, together, load, base, store):
    lane = lanes_of()

    def body(i, carry):
        groups = [load(i * together + u) for u in range(together)]
        groups = [exchange_bits(parts, base, lane) for parts in groups]
        for u, parts in enumerate(groups):
            store(i * together + u, parts)
        return carry

    lax.fori_loop(0, total // together, body, 0)


def lanes_of(rows=16):
    return lax.broadcasted_iota(jnp.int32, (rows, 128), 1)


def cos_sin(value, turn):
    quarter = POINTS // 4
    index = jnp.floor(value * (1.0 / quarter) + 0.5)
    angle = (value - index * quarter) * (2.0 * math.pi / POINTS)
    sq = angle * angle
    c = 1.0 + sq * (-0.5 + sq * (1 / 24 + sq * (-1 / 720 + sq * (1 / 40320))))
    s = angle * (1.0 + sq * (-1 / 6 + sq * (1 / 120 + sq * (-1 / 5040))))
    index = (index.astype(jnp.int32) + turn) & 3
    odd = (index & 1) == 1
    cos = jnp.where(odd, s, c)
    sin = jnp.where(odd, c, s)
    cos = jnp.where((index == 1) | (index == 2), -cos, cos)
    sin = jnp.where(index >= 2, -sin, sin)
    return cos, sin


def make_table(p, wave, part, table, b_cos, b_sin, a_cos, a_sin):
    w = wave[p]
    row = lax.broadcasted_iota(jnp.int32, (128, 512), 0).astype(F32)
    b_cos[...], b_sin[...] = cos_sin(row * w, 0)
    row = lax.broadcasted_iota(jnp.int32, (24, 512), 0).astype(F32)
    a_cos[...], a_sin[...] = cos_sin(row * (128.0 * w), part[p])

    def fill(a, carry):
        values = a_cos[pl.ds(a, 1), :] * b_cos[...] - a_sin[pl.ds(a, 1), :] * b_sin[...]
        table[p, pl.ds(pl.multiple_of(a * 128, 128), 128), :] = values.astype(BF16)
        return carry

    lax.fori_loop(0, POINTS // 128, fill, 0)


def analyse(p, grid, weight, table, y, chunks):
    def field(f, carry):
        base = pl.multiple_of(f * 384, 384)
        values = jnp.dot(grid[pl.ds(base, 384), :], table[p], preferred_element_type=F32)
        for tile in range(4):
            y[tile] = values[:, tile * 128 : tile * 128 + 128] * weight[...]

        def load(n):
            third, tile = n // 4, lax.rem(n, 4)
            return [
                y[tile, pl.ds(third * 128 + l, 16, stride=8), :].astype(BF16) for l in range(8)
            ]

        def store(n, parts):
            third, tile = n // 4, lax.rem(n, 4)
            for e, out in enumerate(parts):
                chunks[9 * p + 3 * f + third, tile * 8 + e] = out

        each(12, 4, load, 1, store)
        return carry

    lax.fori_loop(0, 3, field, 0)


def pack_chunks(t, chunks, send):
    def load(i):
        return [chunks[4 * t + g, i] for g in range(4)]

    def store(i, parts):
        for x, out in enumerate(parts):
            send[4 * i + x, t] = out

    each(BANDS, 8, load, 32, store)


def spread_legendre(p, legendre, slot_row, slot_column, wide, tall):
    wide[p, 768:ROWS, :] = jnp.zeros((16, 1536), BF16)
    tall[p, :, 768:DEPTH] = jnp.zeros((1536, 128), BF16)
    for tile, (low, size) in enumerate(WINDOWS):
        at = tile * 384
        part = legendre[p, :, low : low + size]
        row = lax.broadcasted_iota(jnp.int32, (size, 384), 0) + low
        pick = jnp.where(row == slot_row[:, at : at + 384], 1.0, 0.0).astype(BF16)
        wide[p, 0 : WIDTH + 1, at : at + 384] = jnp.dot(
            part, pick, preferred_element_type=F32
        ).astype(BF16)
        row = lax.broadcasted_iota(jnp.int32, (384, size), 1) + low
        pick = jnp.where(row == slot_column[at : at + 384, :], 1.0, 0.0).astype(BF16)
        tall[p, at : at + 384, 0 : WIDTH + 1] = lax.dot_general(
            pick, part, (((1,), (1,)), ((), ())), preferred_element_type=F32
        ).astype(BF16)


def gather_tiles(t, received, fourier):
    def load(b):
        return [received[4 * b + v, t] for v in range(4)]

    def store(b, parts):
        for g, out in enumerate(parts):
            q = 4 * t + g
            if q < 27:
                f, third = q % 9 // 3, q % 3
                row = pl.multiple_of(b * 48 + third * 16, 16)
                fourier[q // 9, pl.ds(row, 16), f * 128 : f * 128 + 128] = out

    each(BANDS, 8, load, 32, store)


def split_mix(i, mixes, mixers):
    mix = mixes[i]
    high = mix.astype(BF16)
    mixers[i, 0:128, 0:128] = high
    mixers[i, 128:256, 0:128] = high
    mixers[i, 0:128, 128:256] = (mix - high.astype(F32)).astype(BF16)
    mixers[i, 128:256, 128:256] = jnp.zeros((128, 128), BF16)


def mixed(values, mixer):
    high = values.astype(BF16)
    low = (values - high.astype(F32)).astype(BF16)
    out = jnp.dot(
        jnp.concatenate([high, low], axis=1), mixer, preferred_element_type=F32
    )
    return out[:, 0:128] + out[:, 128:256]


def spectral_step(p, own_wave, lane_scales, mixers, wide, tall, fourier, spectral, updated):
    wave = own_wave[p]
    spectral[...] = jnp.dot(wide[p], fourier[p], preferred_element_type=F32)
    upper = (lanes_of(112) & 16) != 0
    updated[ROWS:DEPTH, :] = jnp.zeros((DEPTH - ROWS, 384), BF16)

    def block(i, carry):
        at = pl.multiple_of(i * 112, 112)
        k = lax.broadcasted_iota(jnp.int32, (112, 128), 0) + at
        own = k < WIDTH - wave
        degree = jnp.where(own, wave + k, k - 1)
        ratio = (degree * (degree + 1)).astype(F32) / float(WIDTH * (WIDTH - 1))
        keep = (own != upper) & (k <= WIDTH)
        rows = pl.ds(at, 112)
        first = spectral[rows, 0:128] / (1.0 + lane_scales[0:1, :] * ratio * ratio)
        modes = mixed(spectral[rows, 128:256], mixers[0])
        modes = modes / (1.0 + lane_scales[1:2, :] * ratio)
        second = mixed(modes, mixers[1])
        third = spectral[rows, 256:384] - mixed(second, mixers[2])
        for f, values in enumerate((first, second, third)):
            updated[rows, f * 128 : f * 128 + 128] = jnp.where(keep, values, 0.0).astype(BF16)
        return carry

    lax.fori_loop(0, ROWS // 112, block, 0)
    double = (lax.broadcasted_iota(jnp.int32, (1, 384), 1) & 16 != 0) | (wave > 0)
    factor = jnp.where(double, 2.0, 1.0)

    def rows_of(i, carry):
        at = pl.multiple_of(i * 384, 384)
        values = jnp.dot(tall[p, pl.ds(at, 384), :], updated[...], preferred_element_type=F32)
        fourier[p, pl.ds(at, 384), :] = (values * factor).astype(BF16)
        return carry

    lax.fori_loop(0, 4, rows_of, 0)


def scatter_tiles(t, synthesis, send):
    def load(b):
        parts = []
        for g in range(4):
            q = min(4 * t + g, 26)
            f, third = q % 9 // 3, q % 3
            row = pl.multiple_of(b * 48 + third * 16, 16)
            parts.append(synthesis[q // 9, pl.ds(row, 16), f * 128 : f * 128 + 128])
        return parts

    def store(b, parts):
        for v, out in enumerate(parts):
            send[4 * b + v, t] = out

    each(BANDS, 8, load, 32, store)


def open_tiles(t, received, chunks):
    def load(i):
        return [received[4 * i + x, t] for x in range(4)]

    def store(i, parts):
        for g, out in enumerate(parts):
            if 4 * t + g < 27:
                chunks[4 * t + g, i] = out

    each(BANDS, 8, load, 32, store)


def synthesise(f, chunks, table, y, columns, out):
    def load(n):
        tile, third = n // 3, lax.rem(n, 3)
        p, eighth = tile // 4, lax.rem(tile, 4)
        return [chunks[9 * p + 3 * f + third, eighth * 8 + e] for e in range(8)]

    def store(n, parts):
        tile, third = n // 3, lax.rem(n, 3)
        for l, values in enumerate(parts):
            y[tile, pl.ds(third * 128 + l, 16, stride=8), :] = values.astype(F32)

    each(36, 4, load, 1, store)
    for tile in range(12):
        columns[:, tile * 128 : tile * 128 + 128] = y[tile].astype(BF16)
    base = pl.multiple_of(f * 384, 384)

    def points(i, carry):
        at = pl.multiple_of(i * 256, 256)
        total = jnp.zeros((384, 256), F32)
        for p in range(3):
            total = total + lax.dot_general(
                columns[:, p * 512 : p * 512 + 512],
                table[p, pl.ds(at, 256), :],
                (((1,), (1,)), ((), ())),
                preferred_element_type=F32,
            )
        out[pl.ds(base, 384), pl.ds(at, 256)] = total.astype(BF16)
        return carry

    lax.fori_loop(0, POINTS // 256, points, 0)


PHASES = ((0, 2), (2, 2), (4, 3))


def place():
    lat, lev = lax.axis_index("lat"), lax.axis_index("lev")
    return lat, lev, lat * 4 + lev


def partner(k, lat, lev):
    step = lax.rem(k * 37, 128)
    z = lax.rem(lat // 8 + step // 32, 4)
    y = lax.rem(lat // 2 + step // 8, 4)
    core = lax.rem(lat + step, 2)
    return (z * 4 + y) * 2 + core, lax.rem(lev + step // 2, 4)


def greet_all():
    lat, lev, _ = place()
    barrier = pltpu.get_barrier_semaphore()

    def greet(k, carry):
        pl.semaphore_signal(
            barrier,
            inc=1,
            device_id=partner(k, lat, lev),
            device_id_type=pl.DeviceIdType.MESH,
        )
        return carry

    lax.fori_loop(1, 128, greet, 0)


def launch(phase, send, received, send_sem, recv_sem, own_sem):
    lat, lev, me = place()
    first, count = PHASES[phase]
    tiles = pl.ds(first, count)
    pltpu.make_async_copy(send.at[me, tiles], received.at[me, tiles], own_sem).start()

    def one(k, carry):
        to = partner(k, lat, lev)
        pltpu.make_async_remote_copy(
            src_ref=send.at[to[0] * 4 + to[1], tiles],
            dst_ref=received.at[me, tiles],
            send_sem=send_sem,
            recv_sem=recv_sem,
            device_id=to,
            device_id_type=pl.DeviceIdType.MESH,
        ).start()
        return carry

    lax.fori_loop(1, 128, one, 0)


def rest(phase, send, received, send_sem, recv_sem):
    lat, lev, _ = place()
    first, count = PHASES[phase]
    others = pl.ds(0, 127), pl.ds(first, count)
    return pltpu.make_async_remote_copy(
        src_ref=send.at[others],
        dst_ref=received.at[others],
        send_sem=send_sem,
        recv_sem=recv_sem,
        device_id=(lat, lev),
        device_id_type=pl.DeviceIdType.MESH,
    )


def arrive(phase, send, received, send_sem, recv_sem, own_sem):
    _, _, me = place()
    first, count = PHASES[phase]
    tiles = pl.ds(first, count)
    pltpu.make_async_copy(send.at[me, tiles], received.at[me, tiles], own_sem).wait()
    rest(phase, send, received, send_sem, recv_sem).wait_recv()


def step_kernel(
    grid_hbm, legendre_hbm, wave, part, weight, slot_row, slot_column, own_wave, lane_scales, mixes,
    out_hbm,
    grid, legendre, table, b_cos, b_sin, a_cos, a_sin, y, columns, chunks, send, received, returned,
    wide, tall, fourier, spectral, updated, mixers,
    grid_sem, legendre_sem, out_sem, send_sem, recv_sem, own_sem,
):
    def field_of(ref, f):
        return ref.at[pl.ds(f * 384, 384)]

    for f in range(3):
        pltpu.make_async_copy(field_of(grid_hbm, f), field_of(grid, f), grid_sem.at[f]).start()
    pltpu.make_async_copy(legendre_hbm, legendre, legendre_sem).start()
    greet_all()
    chunks[27] = jnp.zeros(chunks.shape[1:], BF16)
    there = [
        (send, received, send_sem.at[i], recv_sem.at[i], own_sem.at[i]) for i in range(3)
    ]
    back = [
        (send, returned, send_sem.at[3 + i], recv_sem.at[3 + i], own_sem.at[3 + i])
        for i in range(3)
    ]
    for p in range(3):
        make_table(p, wave, part, table, b_cos, b_sin, a_cos, a_sin)
        if p == 0:
            for f in range(3):
                pltpu.make_async_copy(
                    field_of(grid_hbm, f), field_of(grid, f), grid_sem.at[f]
                ).wait()
        analyse(p, grid, weight, table, y, chunks)
        first, count = PHASES[p]
        for t in range(first, first + count):
            pack_chunks(t, chunks, send)
        if p == 0:
            pl.semaphore_wait(pltpu.get_barrier_semaphore(), 127)
        launch(p, *there[p])
    pltpu.make_async_copy(legendre_hbm, legendre, legendre_sem).wait()
    for i in range(3):
        split_mix(i, mixes, mixers)
    for p in range(3):
        spread_legendre(p, legendre, slot_row, slot_column, wide, tall)
    for p in range(3):
        for phase in ((0, 1), (2,), ())[p]:
            arrive(phase, *there[phase])
            first, count = PHASES[phase]
            for t in range(first, first + count):
                gather_tiles(t, received, fourier)
        spectral_step(
            p, own_wave, lane_scales, mixers, wide, tall, fourier, spectral, updated
        )
        rest(p, *there[p][:4]).wait_send()
        first, count = PHASES[p]
        for t in range(first, first + count):
            scatter_tiles(t, fourier, send)
        launch(p, *back[p])
    for phase in range(3):
        arrive(phase, *back[phase])
        first, count = PHASES[phase]
        for t in range(first, first + count):
            open_tiles(t, returned, chunks)
    for f in range(3):
        synthesise(f, chunks, table, y, columns, grid)
        pltpu.make_async_copy(field_of(grid, f), field_of(out_hbm, f), out_sem.at[f]).start()
    for f in range(3):
        pltpu.make_async_copy(field_of(grid, f), field_of(out_hbm, f), out_sem.at[f]).wait()
    for phase in range(3):
        rest(phase, *back[phase][:4]).wait_send()


def step(*inputs):
    vmem = pl.BlockSpec(memory_space=pltpu.VMEM)
    smem = pl.BlockSpec(memory_space=pltpu.SMEM)
    hbm = pl.BlockSpec(memory_space=pl.ANY)
    block = (128, 7, 16, 128)
    scratch = [
        ((1152, POINTS), BF16),
        ((3, WIDTH + 1, NLAT), BF16),
        ((3, POINTS, 512), BF16),
        ((128, 512), F32),
        ((128, 512), F32),
        ((24, 512), F32),
        ((24, 512), F32),
        ((12, 384, 128), F32),
        ((384, 1536), BF16),
        ((28, 32, 16, 128), BF16),
        (block, BF16),
        (block, BF16),
        (block, BF16),
        ((3, ROWS, 1536), BF16),
        ((3, 1536, DEPTH), BF16),
        ((3, 1536, 384), BF16),
        ((ROWS, 384), F32),
        ((DEPTH, 384), BF16),
        ((3, 256, 256), BF16),
    ]
    dma = pltpu.SemaphoreType.DMA
    return pl.pallas_call(
        step_kernel,
        out_shape=jax.ShapeDtypeStruct((1152, POINTS), BF16),
        in_specs=[hbm, hbm, vmem, vmem, vmem, vmem, vmem, smem, vmem, vmem],
        out_specs=hbm,
        scratch_shapes=[pltpu.VMEM(s, d) for s, d in scratch]
        + [dma((3,)), dma, dma((3,)), dma((6,)), dma((6,)), dma((6,))],
        compiler_params=pltpu.CompilerParams(
            vmem_limit_bytes=67043328, collective_id=0, has_side_effects=True
        ),
    )(*inputs)


def shards(
    grid,
    legendre,
    gauss_weights,
    band_counts,
    pair_m,
    vert_modes,
    mode_depth,
    diffusion,
    pressure_balance_matrix,
):
    lev_groups = 4
    fields, lat_cap, lev_dev, points = grid.shape
    my_band = lax.axis_index("lat")
    owner = my_band * lev_groups + lax.axis_index("lev")
    band_starts = jnp.cumsum(band_counts) - band_counts
    offsets = jnp.arange(lat_cap, dtype=jnp.int32)
    slot = jnp.where(
        offsets[None, :] < band_counts[:, None], band_starts[:, None] + offsets[None, :], -1
    ).astype(jnp.int32)
    my_start = lax.dynamic_slice(band_starts, (my_band,), (1,))[0]
    my_count = lax.dynamic_slice(band_counts, (my_band,), (1,))[0]
    padded = jnp.concatenate([gauss_weights, jnp.zeros((lat_cap,), F32)])
    weight = lax.dynamic_slice(padded, (my_start,), (lat_cap,)) * (1.0 / POINTS)
    weight = jnp.where(offsets < my_count, weight, 0.0)
    weight = jnp.broadcast_to(weight[:, None, None], (lat_cap, lev_dev, 128)).reshape(384, 128)

    lower = pair_m.reshape(4, 8, 4, 3).transpose(3, 0, 2, 1)
    waves = jnp.stack([lower, WIDTH - 1 - lower], axis=3)
    waves = jnp.broadcast_to(waves[:, :, :, :, None, :], (3, 4, 4, 2, 2, 8))
    part = jnp.broadcast_to(
        jnp.arange(2, dtype=jnp.int32)[None, None, None, None, :, None], waves.shape
    ).reshape(3, 1, 512)
    waves = waves.reshape(3, 1, 512).astype(F32)
    own_wave = lax.dynamic_slice(pair_m, (owner * 3,), (3,))

    def over_lanes(v):
        v = v.reshape(4, 1, 8)
        return jnp.broadcast_to(v, (4, 4, 8)).reshape(128)

    def mix(m):
        m = m.reshape(4, 1, 8, 4, 1, 8) * jnp.eye(4, dtype=F32).reshape(1, 4, 1, 1, 4, 1)
        return m.reshape(128, 128)

    lane_scales = jnp.stack([over_lanes(diffusion), over_lanes(mode_depth)])
    mixes = jnp.stack([mix(vert_modes.T), mix(vert_modes), mix(pressure_balance_matrix.T)])

    out = step(
        grid.reshape(1152, points),
        legendre,
        waves,
        part,
        weight,
        slot.reshape(1, 1536),
        slot.reshape(1536, 1),
        own_wave,
        lane_scales,
        mixes,
    )
    return out.reshape(fields, lat_cap, lev_dev, points)


def solution(mesh):
    placed = (
        P(None, "lat", "lev", None),
        P(("lat", "lev"), None, None),
        P(),
        P(),
        P(),
        P(),
        P(),
        P(),
        P(),
    )
    return jax.shard_map(
        shards, mesh=mesh, in_specs=placed, out_specs=P(None, "lat", "lev", None), check_vma=False
    )
```

```python
import math

import jax
import jax.numpy as jnp
from jax import lax
from jax.experimental import pallas as pl
from jax.experimental.pallas import tpu as pltpu
from jax.sharding import PartitionSpec as P

WIDTH = 768
NLAT = 1280
POINTS = 2816
ROWS = 784
DEPTH = 896
BANDS = 32
F32, BF16 = jnp.float32, jnp.bfloat16

WINDOWS = ((0, 384), (128, 640), (512, 640), (896, 384))


def swap(a, b, bit, low):
    return (
        jnp.where(low, a, pltpu.roll(b, bit, 1)),
        jnp.where(low, pltpu.roll(a, 128 - bit, 1), b),
    )


def exchange_bits(arrays, base, lane):
    arrays = list(arrays)
    step = 1
    while step < len(arrays):
        bit = base * step
        low = (lane & bit) == 0
        for i in range(len(arrays)):
            if not i & step:
                arrays[i], arrays[i | step] = swap(arrays[i], arrays[i | step], bit, low)
        step *= 2
    return arrays


def each(total, together, load, base, store):
    lane = lanes_of()

    def body(i, carry):
        groups = [load(i * together + u) for u in range(together)]
        groups = [exchange_bits(parts, base, lane) for parts in groups]
        for u, parts in enumerate(groups):
            store(i * together + u, parts)
        return carry

    lax.fori_loop(0, total // together, body, 0)


def lanes_of(rows=16):
    return lax.broadcasted_iota(jnp.int32, (rows, 128), 1)


def cos_sin(value, turn):
    quarter = POINTS // 4
    index = jnp.floor(value * (1.0 / quarter) + 0.5)
    angle = (value - index * quarter) * (2.0 * math.pi / POINTS)
    sq = angle * angle
    c = 1.0 + sq * (-0.5 + sq * (1 / 24 + sq * (-1 / 720 + sq * (1 / 40320))))
    s = angle * (1.0 + sq * (-1 / 6 + sq * (1 / 120 + sq * (-1 / 5040))))
    index = (index.astype(jnp.int32) + turn) & 3
    odd = (index & 1) == 1
    cos = jnp.where(odd, s, c)
    sin = jnp.where(odd, c, s)
    cos = jnp.where((index == 1) | (index == 2), -cos, cos)
    sin = jnp.where(index >= 2, -sin, sin)
    return cos, sin


def make_table(p, pairs, table, wave, b_cos, b_sin, a_cos, a_sin):
    lane = lax.broadcasted_iota(jnp.int32, (128, 128), 1)
    device = lax.broadcasted_iota(jnp.int32, (128, 128), 0)
    lower = pairs[:, p : p + 1].astype(F32)
    upper = (lanes_of(1) & 16) != 0
    for tile in range(4):
        chosen = device == 32 * tile + 4 * (lane & 7) + (lane >> 5)
        low = jnp.sum(jnp.where(chosen, lower, 0.0), axis=0, keepdims=True)
        wave[:, tile * 128 : tile * 128 + 128] = jnp.where(upper, WIDTH - 1 - low, low)
    w = wave[...]
    row = lax.broadcasted_iota(jnp.int32, (128, 512), 0).astype(F32)
    b_cos[...], b_sin[...] = cos_sin(row * w, 0)
    row = lax.broadcasted_iota(jnp.int32, (24, 512), 0).astype(F32)
    part = (lax.broadcasted_iota(jnp.int32, (24, 512), 1) >> 3) & 1
    a_cos[...], a_sin[...] = cos_sin(row * (128.0 * w), part)

    def fill(a, carry):
        values = a_cos[pl.ds(a, 1), :] * b_cos[...] - a_sin[pl.ds(a, 1), :] * b_sin[...]
        rows = pl.ds(pl.multiple_of(a * 128, 128), 128)
        table[rows, p * 512 : p * 512 + 512] = values.astype(BF16)
        return carry

    lax.fori_loop(0, POINTS // 128, fill, 0)


def analyse(p, grid, weight, table, y, chunks):
    def field(f, carry):
        base = pl.multiple_of(f * 384, 384)
        values = jnp.dot(
            grid[pl.ds(base, 384), :],
            table[:, p * 512 : p * 512 + 512],
            preferred_element_type=F32,
        )
        for tile in range(4):
            y[tile] = values[:, tile * 128 : tile * 128 + 128] * weight[...]

        def load(n):
            third, tile = n // 4, lax.rem(n, 4)
            return [
                y[tile, pl.ds(third * 128 + l, 16, stride=8), :].astype(BF16) for l in range(8)
            ]

        def store(n, parts):
            third, tile = n // 4, lax.rem(n, 4)
            for e, out in enumerate(parts):
                chunks[9 * p + 3 * f + third, tile * 8 + e] = out

        each(12, 4, load, 1, store)
        return carry

    lax.fori_loop(0, 3, field, 0)


def crossed(parts, cross):
    whole = jnp.concatenate([part.reshape(512, 128) for part in parts], axis=1)
    out = jnp.dot(whole, cross[...], preferred_element_type=F32).astype(BF16)
    return [out[:, i * 128 : i * 128 + 128].reshape(32, 16, 128) for i in range(4)]


def fours(i):
    return pl.ds(32 * i, 32)


def pack_chunks(t, chunks, cross, send):
    for x, out in enumerate(crossed([chunks[4 * t + g] for g in range(4)], cross)):
        send[fours(x), t] = out


def make_cross(cross):
    source = lax.broadcasted_iota(jnp.int32, (512, 512), 0)
    target = lax.broadcasted_iota(jnp.int32, (512, 512), 1)
    from_lane = ((source >> 5) & 3) * 128 + (source >> 7) * 32 + (source & 31)
    cross[...] = jnp.where(from_lane == target, 1.0, 0.0).astype(BF16)


def spread_legendre(p, legendre, slot_row, slot_column, wide, tall):
    wide[p * ROWS + 768 : p * ROWS + ROWS, :] = jnp.zeros((16, 1536), BF16)
    tall[p, :, 768:DEPTH] = jnp.zeros((1536, 128), BF16)
    for tile, (low, size) in enumerate(WINDOWS):
        at = tile * 384
        part = legendre[p, :, low : low + size]
        row = lax.broadcasted_iota(jnp.int32, (size, 384), 0) + low
        pick = jnp.where(row == slot_row[:, at : at + 384], 1.0, 0.0).astype(BF16)
        wide[p * ROWS : p * ROWS + WIDTH + 1, at : at + 384] = jnp.dot(
            part, pick, preferred_element_type=F32
        ).astype(BF16)
        row = lax.broadcasted_iota(jnp.int32, (384, size), 1) + low
        pick = jnp.where(row == slot_column[at : at + 384, :], 1.0, 0.0).astype(BF16)
        tall[p, at : at + 384, 0 : WIDTH + 1] = lax.dot_general(
            pick, part, (((1,), (1,)), ((), ())), preferred_element_type=F32
        ).astype(BF16)


def gather_tiles(t, received, cross, fourier):
    for g, out in enumerate(crossed([received[fours(v), t] for v in range(4)], cross)):
        q = 4 * t + g
        if q < 27:
            f, third = q % 9 // 3, q % 3
            fourier[q // 9, :, third, :, f * 128 : f * 128 + 128] = out


def mixed(values, mixer):
    high = values.astype(BF16)
    low = (values - high.astype(F32)).astype(BF16)
    out = jnp.dot(
        jnp.concatenate([high, low], axis=1), mixer, preferred_element_type=F32
    )
    return out[:, 0:128] + out[:, 128:256]


def spectral_step(p, wave, lane_scales, mixers, wide, tall, fourier, spectral, updated):
    spectral[...] = jnp.dot(
        wide[p * ROWS : p * ROWS + ROWS, :],
        fourier[p].reshape(1536, 384),
        preferred_element_type=F32,
    )
    updated[ROWS:DEPTH, :] = jnp.zeros((DEPTH - ROWS, 384), BF16)
    for at, size in ((0, 400), (400, 384)):
        k = lax.broadcasted_iota(jnp.int32, (size, 128), 0) + at
        own = k < WIDTH - wave
        degree = jnp.where(own, wave + k, k - 1)
        ratio = (degree * (degree + 1)).astype(F32) * (1.0 / float(WIDTH * (WIDTH - 1)))
        keep = (own != ((lanes_of(size) & 16) != 0)) & (k <= WIDTH)
        rows = slice(at, at + size)
        first = spectral[rows, 0:128] / (1.0 + lane_scales[0:1, :] * ratio * ratio)
        modes = mixed(spectral[rows, 128:256], mixers[0])
        modes = modes / (1.0 + lane_scales[1:2, :] * ratio)
        second = mixed(modes, mixers[1])
        third = spectral[rows, 256:384] - mixed(second, mixers[2])
        for f, values in enumerate((first, second, third)):
            updated[rows, f * 128 : f * 128 + 128] = jnp.where(keep, values, 0.0).astype(BF16)
    double = (lax.broadcasted_iota(jnp.int32, (1, 384), 1) & 16 != 0) | (wave > 0)
    factor = jnp.where(double, 2.0, 1.0)

    def rows_of(i, carry):
        at = pl.multiple_of(i * 384, 384)
        values = jnp.dot(tall[p, pl.ds(at, 384), :], updated[...], preferred_element_type=F32)
        out = (values * factor).astype(BF16)
        fourier[p, pl.ds(pl.multiple_of(i * 8, 8), 8)] = out.reshape(8, 3, 16, 384)
        return carry

    lax.fori_loop(0, 4, rows_of, 0)


def scatter_tiles(t, synthesis, cross, send):
    parts = []
    for q in range(4 * t, 4 * t + 4):
        q = min(q, 26)
        f, third = q % 9 // 3, q % 3
        parts.append(synthesis[q // 9, :, third, :, f * 128 : f * 128 + 128])
    for v, out in enumerate(crossed(parts, cross)):
        send[fours(v), t] = out


def open_tiles(t, received, cross, chunks):
    for g, out in enumerate(crossed([received[fours(x), t] for x in range(4)], cross)):
        if 4 * t + g < 27:
            chunks[4 * t + g] = out


def arrange(p, f, chunks, y, columns):
    def load(n):
        third, tile = n // 4, lax.rem(n, 4)
        return [chunks[9 * p + 3 * f + third, tile * 8 + e] for e in range(8)]

    def store(n, parts):
        third, tile = n // 4, lax.rem(n, 4)
        for l, values in enumerate(parts):
            y[tile, pl.ds(third * 128 + l, 16, stride=8), :] = values.astype(F32)

    each(12, 4, load, 1, store)
    for tile in range(4):
        at = p * 512 + tile * 128
        columns[f * 384 : f * 384 + 384, at : at + 128] = y[tile].astype(BF16)


def synthesise(i, columns, table, out):
    at = pl.multiple_of(i * 256, 256)
    out[:, pl.ds(at, 256)] = lax.dot_general(
        columns[...],
        table[pl.ds(at, 256), :],
        (((1,), (1,)), ((), ())),
        preferred_element_type=F32,
    ).astype(BF16)


def prepare(band_counts, gauss, weight, slot_row, slot_column):
    lat = lax.axis_index("lat")
    place_ = lax.broadcasted_iota(jnp.int32, (1, 1536), 1)
    offset = lax.broadcasted_iota(jnp.int32, (48, 1), 0)
    row = jnp.full((1, 1536), -1, jnp.int32)
    start, mine, count = 0, 0, 0
    for b in range(BANDS):
        size = band_counts[b]
        inside = place_ - 48 * b
        row = jnp.where((inside >= 0) & (inside < size), start + inside, row)
        slot_column[48 * b : 48 * b + 48, :] = jnp.where(offset < size, start + offset, -1)
        mine = mine + jnp.where(b < lat, size, 0)
        count = count + jnp.where(b == lat, size, 0)
        start = start + size
    slot_row[...] = row
    wanted = jnp.where(offset < count, mine + offset, -1)
    column = lax.broadcasted_iota(jnp.int32, (48, NLAT), 1)
    chosen = jnp.where(column == wanted, gauss[...], 0.0)
    values = jnp.sum(chosen, axis=1, keepdims=True) * (1.0 / POINTS)
    for r in range(48):
        weight[8 * r : 8 * r + 8, :] = jnp.broadcast_to(values[r : r + 1, :], (8, 128))


def over_lanes(row, spread):
    return lax.dot_general(
        row,
        spread,
        (((1,), (1,)), ((), ())),
        precision=lax.Precision.HIGHEST,
        preferred_element_type=F32,
    )


def make_mixers(vert_modes, mode_depth, diffusion, balance, lane_scales, mixers):
    lane = lax.broadcasted_iota(jnp.int32, (128, 32), 0)
    level = lax.broadcasted_iota(jnp.int32, (128, 32), 1)
    spread = jnp.where((lane >> 5) * 8 + (lane & 7) == level, 1.0, 0.0)
    lane_scales[0:1, :] = over_lanes(diffusion[...], spread)
    lane_scales[1:2, :] = over_lanes(mode_depth[...], spread)
    spread = spread.astype(BF16)
    one = (lax.broadcasted_iota(jnp.int32, (128, 128), 0) >> 3) & 3
    two = (lax.broadcasted_iota(jnp.int32, (128, 128), 1) >> 3) & 3

    def widen(m, side):
        half = lax.dot_general(
            spread, m, (((1,), (side,)), ((), ())), preferred_element_type=F32
        ).astype(BF16)
        full = lax.dot_general(
            half, spread, (((1,), (1,)), ((), ())), preferred_element_type=F32
        )
        return jnp.where(one == two, full, 0.0).astype(BF16)

    for i, (m, side) in enumerate(((vert_modes, 1), (vert_modes, 0), (balance, 1))):
        high = m[...].astype(BF16)
        low = (m[...] - high.astype(F32)).astype(BF16)
        wide_high = widen(high, side)
        mixers[i, 0:128, 0:128] = wide_high
        mixers[i, 128:256, 0:128] = wide_high
        mixers[i, 0:128, 128:256] = widen(low, side)
        mixers[i, 128:256, 128:256] = jnp.zeros((128, 128), BF16)


PHASES = ((0, 2), (2, 2), (4, 3))


def place():
    lat, lev = lax.axis_index("lat"), lax.axis_index("lev")
    return lat, lev, lev * 32 + lat


def partners():
    lat, lev, _ = place()
    zs = [lax.rem(lat // 8 + i, 4) * 8 for i in range(4)]
    ys = [lax.rem(lat // 2 + i, 4) * 2 for i in range(4)]
    cores = [lax.rem(lat + i, 2) for i in range(2)]
    levs = [lax.rem(lev + i, 4) for i in range(4)]
    for k in range(1, 128):
        step = k * 37 % 128
        yield zs[step // 32] + ys[step // 8 % 4] + cores[step % 2], levs[step // 2 % 4]


def greet_all():
    barrier = pltpu.get_barrier_semaphore()
    for to in partners():
        pl.semaphore_signal(
            barrier, inc=1, device_id=to, device_id_type=pl.DeviceIdType.MESH
        )


def hear_all():
    pl.semaphore_wait(pltpu.get_barrier_semaphore(), 127)


def launch(phase, send, received, send_sem, recv_sem, own_sem):
    _, _, me = place()
    first, count = PHASES[phase]
    tiles = pl.ds(first, count)
    pltpu.make_async_copy(send.at[me, tiles], received.at[me, tiles], own_sem).start()
    for to in partners():
        pltpu.make_async_remote_copy(
            src_ref=send.at[to[1] * 32 + to[0], tiles],
            dst_ref=received.at[me, tiles],
            send_sem=send_sem,
            recv_sem=recv_sem,
            device_id=to,
            device_id_type=pl.DeviceIdType.MESH,
        ).start()


def rest(phase, send, received, send_sem, recv_sem):
    lat, lev, _ = place()
    first, count = PHASES[phase]
    others = pl.ds(0, 127), pl.ds(first, count)
    return pltpu.make_async_remote_copy(
        src_ref=send.at[others],
        dst_ref=received.at[others],
        send_sem=send_sem,
        recv_sem=recv_sem,
        device_id=(lat, lev),
        device_id_type=pl.DeviceIdType.MESH,
    )


def arrive(phase, send, received, send_sem, recv_sem, own_sem):
    _, _, me = place()
    first, count = PHASES[phase]
    tiles = pl.ds(first, count)
    pltpu.make_async_copy(send.at[me, tiles], received.at[me, tiles], own_sem).wait()
    rest(phase, send, received, send_sem, recv_sem).wait_recv()


def wait_sent(phase, send, received, send_sem, recv_sem, own_sem):
    rest(phase, send, received, send_sem, recv_sem).wait_send()


def tiles_of(phase):
    first, count = PHASES[phase]
    return range(first, first + count)


def step_kernel(
    grid_hbm, legendre_hbm, pairs, pair_m, band_counts, gauss, vert_modes, mode_depth, diffusion,
    balance, out_hbm,
    grid, legendre, table, wave, b_cos, b_sin, a_cos, a_sin, y, chunks,
    send, received, returned, wide, tall, fourier, spectral, updated, mixers, cross,
    weight, slot_row, slot_column, lane_scales,
    grid_sem, legendre_sem, out_sem, send_sem, recv_sem, own_sem,
):
    def field_of(ref, f):
        return ref.at[pl.ds(f * 384, 384)]

    for f in range(3):
        pltpu.make_async_copy(field_of(grid_hbm, f), field_of(grid, f), grid_sem.at[f]).start()
    pltpu.make_async_copy(legendre_hbm, legendre, legendre_sem).start()
    greet_all()
    chunks[27] = jnp.zeros(chunks.shape[1:], BF16)
    there = [
        (send, received, send_sem.at[i], recv_sem.at[i], own_sem.at[i]) for i in range(3)
    ]
    back = [
        (send, returned, send_sem.at[3 + i], recv_sem.at[3 + i], own_sem.at[3 + i])
        for i in range(3)
    ]
    make_cross(cross)
    prepare(band_counts, gauss, weight, slot_row, slot_column)
    for p in range(3):
        make_table(p, pairs, table, wave, b_cos, b_sin, a_cos, a_sin)
        if p == 0:
            for f in range(3):
                pltpu.make_async_copy(
                    field_of(grid_hbm, f), field_of(grid, f), grid_sem.at[f]
                ).wait()
        analyse(p, grid, weight, table, y, chunks)
        for t in tiles_of(p):
            pack_chunks(t, chunks, cross, send)
        if p == 0:
            hear_all()
        launch(p, *there[p])
    pltpu.make_async_copy(legendre_hbm, legendre, legendre_sem).wait()
    make_mixers(vert_modes, mode_depth, diffusion, balance, lane_scales, mixers)
    lat, lev, _ = place()
    spread_legendre(0, legendre, slot_row, slot_column, wide, tall)
    for p in range(3):
        for phase in ((0, 1), (2,), ())[p]:
            arrive(phase, *there[phase])
            for t in tiles_of(phase):
                gather_tiles(t, received, cross, fourier)
        spectral_step(
            p, pair_m[3 * (4 * lat + lev) + p], lane_scales, mixers, wide, tall, fourier, spectral, updated
        )
        wait_sent(p, *there[p])
        for t in tiles_of(p):
            scatter_tiles(t, fourier, cross, send)
        launch(p, *back[p])
        if p == 0:
            for other in (1, 2):
                spread_legendre(other, legendre, slot_row, slot_column, wide, tall)
    columns = wide.at[0:1152]
    done = 0
    for phase in range(3):
        arrive(phase, *back[phase])
        for t in tiles_of(phase):
            open_tiles(t, returned, cross, chunks)
        ready = min(4 * (tiles_of(phase)[-1] + 1), 27) // 3
        for unit in range(done, ready):
            arrange(unit // 3, unit % 3, chunks, y, columns)
        done = ready

    def part_of(ref, i):
        return ref.at[:, pl.ds(pl.multiple_of(i * 256, 256), 256)]

    def points(i, carry):
        synthesise(i, columns, table, grid)
        pltpu.make_async_copy(part_of(grid, i), part_of(out_hbm, i), out_sem).start()
        return carry

    lax.fori_loop(0, POINTS // 256, points, 0)
    pltpu.make_async_copy(grid, out_hbm, out_sem).wait()
    for phase in range(3):
        wait_sent(phase, *back[phase])


def step(*inputs):
    vmem = pl.BlockSpec(memory_space=pltpu.VMEM)
    smem = pl.BlockSpec(memory_space=pltpu.SMEM)
    hbm = pl.BlockSpec(memory_space=pl.ANY)
    block = (128, 7, 16, 128)
    scratch = [
        ((1152, POINTS), BF16),
        ((3, WIDTH + 1, NLAT), BF16),
        ((POINTS, 1536), BF16),
        ((1, 512), F32),
        ((128, 512), F32),
        ((128, 512), F32),
        ((24, 512), F32),
        ((24, 512), F32),
        ((4, 384, 128), F32),
        ((28, 32, 16, 128), BF16),
        (block, BF16),
        (block, BF16),
        (block, BF16),
        ((3 * ROWS, 1536), BF16),
        ((3, 1536, DEPTH), BF16),
        ((3, 32, 3, 16, 384), BF16),
        ((ROWS, 384), F32),
        ((DEPTH, 384), BF16),
        ((3, 256, 256), BF16),
        ((512, 512), BF16),
        ((384, 128), F32),
        ((1, 1536), jnp.int32),
        ((1536, 1), jnp.int32),
        ((2, 128), F32),
    ]
    dma = pltpu.SemaphoreType.DMA
    return pl.pallas_call(
        step_kernel,
        out_shape=jax.ShapeDtypeStruct((1152, POINTS), BF16),
        in_specs=[hbm, hbm, vmem, smem, smem] + [vmem] * 5,
        out_specs=hbm,
        scratch_shapes=[pltpu.VMEM(s, d) for s, d in scratch]
        + [dma((3,)), dma, dma, dma((6,)), dma((6,)), dma((6,))],
        compiler_params=pltpu.CompilerParams(
            vmem_limit_bytes=67043328, collective_id=0, has_side_effects=True
        ),
    )(*inputs)


def shards(
    grid,
    legendre,
    gauss_weights,
    band_counts,
    pair_m,
    vert_modes,
    mode_depth,
    diffusion,
    pressure_balance_matrix,
):
    fields, lat_cap, lev_dev, points = grid.shape
    out = step(
        grid.reshape(fields * lat_cap * lev_dev, points),
        legendre,
        pair_m.reshape(128, 3),
        pair_m,
        band_counts,
        gauss_weights.reshape(1, NLAT),
        vert_modes,
        mode_depth.reshape(1, 32),
        diffusion.reshape(1, 32),
        pressure_balance_matrix,
    )
    return out.reshape(fields, lat_cap, lev_dev, points)


def solution(mesh):
    placed = (
        P(None, "lat", "lev", None),
        P(("lat", "lev"), None, None),
        P(),
        P(),
        P(),
        P(),
        P(),
        P(),
        P(),
    )
    return jax.shard_map(
        shards, mesh=mesh, in_specs=placed, out_specs=P(None, "lat", "lev", None), check_vma=False
    )
```

```python
import math

import jax
import jax.numpy as jnp
from jax import lax
from jax.experimental import pallas as pl
from jax.experimental.pallas import tpu as pltpu
from jax.sharding import PartitionSpec as P

WIDTH = 768
NLAT = 1280
POINTS = 2816
ROWS = 784
DEPTH = 896
BANDS = 32
F32, BF16 = jnp.float32, jnp.bfloat16

WINDOWS = ((0, 384), (128, 640), (512, 640), (896, 384))


def swap(a, b, bit, low):
    return (
        jnp.where(low, a, pltpu.roll(b, bit, 1)),
        jnp.where(low, pltpu.roll(a, 128 - bit, 1), b),
    )


def exchange_bits(arrays, base, lane):
    arrays = list(arrays)
    step = 1
    while step < len(arrays):
        bit = base * step
        low = (lane & bit) == 0
        for i in range(len(arrays)):
            if not i & step:
                arrays[i], arrays[i | step] = swap(arrays[i], arrays[i | step], bit, low)
        step *= 2
    return arrays


def each(total, together, load, base, store):
    lane = lanes_of()

    def body(i, carry):
        groups = [load(i * together + u) for u in range(together)]
        groups = [exchange_bits(parts, base, lane) for parts in groups]
        for u, parts in enumerate(groups):
            store(i * together + u, parts)
        return carry

    lax.fori_loop(0, total // together, body, 0)


def lanes_of(rows=16):
    return lax.broadcasted_iota(jnp.int32, (rows, 128), 1)


def cos_sin(value, turn):
    quarter = POINTS // 4
    index = jnp.floor(value * (1.0 / quarter) + 0.5)
    angle = (value - index * quarter) * (2.0 * math.pi / POINTS)
    sq = angle * angle
    c = 1.0 + sq * (-0.5 + sq * (1 / 24 + sq * (-1 / 720 + sq * (1 / 40320))))
    s = angle * (1.0 + sq * (-1 / 6 + sq * (1 / 120 + sq * (-1 / 5040))))
    index = (index.astype(jnp.int32) + turn) & 3
    odd = (index & 1) == 1
    cos = jnp.where(odd, s, c)
    sin = jnp.where(odd, c, s)
    cos = jnp.where((index == 1) | (index == 2), -cos, cos)
    sin = jnp.where(index >= 2, -sin, sin)
    return cos, sin


def make_table(p, pairs, table, wave, b_cos, b_sin, a_cos, a_sin):
    lane = lax.broadcasted_iota(jnp.int32, (128, 128), 1)
    device = lax.broadcasted_iota(jnp.int32, (128, 128), 0)
    lane384 = lax.broadcasted_iota(jnp.int32, (128, 384), 1)
    device384 = lax.broadcasted_iota(jnp.int32, (128, 384), 0)
    pair = pairs[...].reshape(1, 384).astype(F32)
    lower = jnp.where(lane384 == 3 * device384 + p, pair, 0.0)
    lower = jnp.sum(lower, axis=1, keepdims=True)
    upper = (lanes_of(1) & 16) != 0
    for tile in range(4):
        chosen = device == 32 * tile + 4 * (lane & 7) + (lane >> 5)
        low = jnp.sum(jnp.where(chosen, lower, 0.0), axis=0, keepdims=True)
        wave[:, tile * 128 : tile * 128 + 128] = jnp.where(upper, WIDTH - 1 - low, low)
    w = wave[...]
    row = lax.broadcasted_iota(jnp.int32, (128, 512), 0).astype(F32)
    b_cos[...], b_sin[...] = cos_sin(row * w, 0)
    row = lax.broadcasted_iota(jnp.int32, (24, 512), 0).astype(F32)
    part = (lax.broadcasted_iota(jnp.int32, (24, 512), 1) >> 3) & 1
    a_cos[...], a_sin[...] = cos_sin(row * (128.0 * w), part)

    def fill(a, carry):
        values = a_cos[pl.ds(a, 1), :] * b_cos[...] - a_sin[pl.ds(a, 1), :] * b_sin[...]
        rows = pl.ds(pl.multiple_of(a * 128, 128), 128)
        table[rows, p * 512 : p * 512 + 512] = values.astype(BF16)
        return carry

    lax.fori_loop(0, POINTS // 128, fill, 0)


def analyse(p, grid, weight, table, y, stage, turn, chunks):
    def field(f, carry):
        base = pl.multiple_of(f * 384, 384)
        values = jnp.dot(
            grid[pl.ds(base, 384), :],
            table[:, p * 512 : p * 512 + 512],
            preferred_element_type=F32,
        )
        for tile in range(4):
            y[tile] = values[:, tile * 128 : tile * 128 + 128] * weight[...]

        for third in range(3):
            for tile in range(4):
                at = pl.multiple_of(f * 192 + (4 * third + tile) * 16, 16)
                for l in range(8):
                    stage[pl.ds(at, 16), l * 128 : l * 128 + 128] = y[
                        tile, pl.ds(third * 128 + l, 16, stride=8), :
                    ].astype(BF16)
        return carry

    lax.fori_loop(0, 3, field, 0)
    chunks[p * 576 : p * 576 + 576, :] = jnp.dot(
        stage[0:576, 0:1024], turn[...], preferred_element_type=F32
    ).astype(BF16)


def crossed(parts, cross):
    whole = jnp.concatenate([part.reshape(512, 128) for part in parts], axis=1)
    out = jnp.dot(whole, cross[...], preferred_element_type=F32).astype(BF16)
    return [out[:, i * 128 : i * 128 + 128].reshape(32, 16, 128) for i in range(4)]


def fours(i):
    return pl.ds(32 * i, 32)


def pack_chunks(t, chunks, cross, send):
    parts = []
    for g in range(4):
        rows = chunks[pl.ds(pl.multiple_of(t * 256 + g * 64, 64), 64), :]
        parts.append(
            jnp.concatenate([rows[:, e * 128 : e * 128 + 128] for e in range(8)], axis=0)
        )
    for x, out in enumerate(crossed(parts, cross)):
        send[fours(x), t] = out


def make_turn(turn):
    source = lax.broadcasted_iota(jnp.int32, (1024, 128), 0)
    target = lax.broadcasted_iota(jnp.int32, (1024, 128), 1)
    for e in range(8):
        from_lane = (target & 7) * 128 + (target >> 3) * 8 + e
        turn[:, e * 128 : e * 128 + 128] = jnp.where(source == from_lane, 1.0, 0.0).astype(BF16)


def make_cross(cross):
    source = lax.broadcasted_iota(jnp.int32, (512, 512), 0)
    target = lax.broadcasted_iota(jnp.int32, (512, 512), 1)
    from_lane = ((source >> 5) & 3) * 128 + (source >> 7) * 32 + (source & 31)
    cross[...] = jnp.where(from_lane == target, 1.0, 0.0).astype(BF16)


def spread_legendre(p, legendre, slot_row, slot_column, wide, tall):
    base = p * ROWS if isinstance(p, int) else pl.multiple_of(p * ROWS, 16)
    wide[pl.ds(base + 768, 16), :] = jnp.zeros((16, 1536), BF16)
    tall[p, :, 768:DEPTH] = jnp.zeros((1536, 128), BF16)
    for tile, (low, size) in enumerate(WINDOWS):
        at = tile * 384
        part = legendre[p, :, low : low + size]
        row = lax.broadcasted_iota(jnp.int32, (size, 384), 0) + low
        pick = jnp.where(row == slot_row[:, at : at + 384], 1.0, 0.0).astype(BF16)
        wide[pl.ds(base, WIDTH + 1), at : at + 384] = jnp.dot(
            part, pick, preferred_element_type=F32
        ).astype(BF16)
        row = lax.broadcasted_iota(jnp.int32, (384, size), 1) + low
        pick = jnp.where(row == slot_column[at : at + 384, :], 1.0, 0.0).astype(BF16)
        tall[p, at : at + 384, 0 : WIDTH + 1] = lax.dot_general(
            pick, part, (((1,), (1,)), ((), ())), preferred_element_type=F32
        ).astype(BF16)


def gather_tiles(t, received, cross, fourier):
    for g, out in enumerate(crossed([received[fours(v), t] for v in range(4)], cross)):
        q = 4 * t + g
        if q < 27:
            f, third = q % 9 // 3, q % 3
            fourier[q // 9, :, third, :, f * 128 : f * 128 + 128] = out


def mixed(values, mixer):
    high = values.astype(BF16)
    low = (values - high.astype(F32)).astype(BF16)
    out = jnp.dot(
        jnp.concatenate([high, low], axis=1), mixer, preferred_element_type=F32
    )
    return out[:, 0:128] + out[:, 128:256]


def spectral_step(p, wave, lane_scales, mixers, wide, tall, fourier, spectral, updated):
    spectral[...] = jnp.dot(
        wide[p * ROWS : p * ROWS + ROWS, :],
        fourier[p].reshape(1536, 384),
        preferred_element_type=F32,
    )
    updated[ROWS:DEPTH, :] = jnp.zeros((DEPTH - ROWS, 384), BF16)
    for at, size in ((0, 400), (400, 384)):
        k = lax.broadcasted_iota(jnp.int32, (size, 128), 0) + at
        own = k < WIDTH - wave
        degree = jnp.where(own, wave + k, k - 1)
        ratio = (degree * (degree + 1)).astype(F32) * (1.0 / float(WIDTH * (WIDTH - 1)))
        keep = (own != ((lanes_of(size) & 16) != 0)) & (k <= WIDTH)
        rows = slice(at, at + size)
        first = spectral[rows, 0:128] / (1.0 + lane_scales[0:1, :] * ratio * ratio)
        modes = mixed(spectral[rows, 128:256], mixers[0])
        modes = modes / (1.0 + lane_scales[1:2, :] * ratio)
        second = mixed(modes, mixers[1])
        third = spectral[rows, 256:384] - mixed(second, mixers[2])
        for f, values in enumerate((first, second, third)):
            updated[rows, f * 128 : f * 128 + 128] = jnp.where(keep, values, 0.0).astype(BF16)
    double = (lax.broadcasted_iota(jnp.int32, (1, 384), 1) & 16 != 0) | (wave > 0)
    factor = jnp.where(double, 2.0, 1.0)

    def rows_of(i, carry):
        at = pl.multiple_of(i * 384, 384)
        values = jnp.dot(tall[p, pl.ds(at, 384), :], updated[...], preferred_element_type=F32)
        out = (values * factor).astype(BF16)
        fourier[p, pl.ds(pl.multiple_of(i * 8, 8), 8)] = out.reshape(8, 3, 16, 384)
        return carry

    lax.fori_loop(0, 4, rows_of, 0)


def scatter_tiles(t, synthesis, cross, send):
    parts = []
    for q in range(4 * t, 4 * t + 4):
        q = min(q, 26)
        f, third = q % 9 // 3, q % 3
        parts.append(synthesis[q // 9, :, third, :, f * 128 : f * 128 + 128])
    for v, out in enumerate(crossed(parts, cross)):
        send[fours(v), t] = out


def open_tiles(t, received, cross, chunks):
    for g, out in enumerate(crossed([received[fours(x), t] for x in range(4)], cross)):
        rows = pl.ds(pl.multiple_of(t * 256 + g * 64, 64), 64)
        out = out.reshape(512, 128)
        for e in range(8):
            chunks[rows, e * 128 : e * 128 + 128] = out[e * 64 : e * 64 + 64]


def arrange(p, f, chunks, y, columns):
    def load(n):
        third, tile = n // 4, lax.rem(n, 4)
        at = pl.multiple_of((9 * p + 3 * f + third) * 64 + tile * 16, 16)
        return [chunks[pl.ds(at, 16), e * 128 : e * 128 + 128] for e in range(8)]

    def store(n, parts):
        third, tile = n // 4, lax.rem(n, 4)
        for l, values in enumerate(parts):
            y[tile, pl.ds(third * 128 + l, 16, stride=8), :] = values.astype(F32)

    each(12, 4, load, 1, store)
    for tile in range(4):
        at = p * 512 + tile * 128
        columns[f * 384 : f * 384 + 384, at : at + 128] = y[tile].astype(BF16)


def synthesise(i, rows, low, high, columns, table, out, add):
    at = pl.ds(pl.multiple_of(i * 256, 256), 256)
    values = lax.dot_general(
        columns[rows, low:high],
        table[at, low:high],
        (((1,), (1,)), ((), ())),
        preferred_element_type=F32,
    )
    if add:
        values = values + out[rows, at].astype(F32)
    out[rows, at] = values.astype(BF16)


def row_weights(band_counts, gauss, weight):
    lat = lax.axis_index("lat")
    start, count = 0, 0
    for b in range(BANDS):
        size = band_counts[b]
        start = start + jnp.where(b < lat, size, 0)
        count = count + jnp.where(b == lat, size, 0)
    for r in range(48):
        value = gauss[jnp.minimum(start + r, NLAT - 1)] * (1.0 / POINTS)
        value = jnp.where(r < count, value, 0.0)
        weight[8 * r : 8 * r + 8, :] = jnp.broadcast_to(value, (8, 128))


def slot_latitudes(band_counts, slot_row, slot_column):
    slot = lax.broadcasted_iota(jnp.int32, (1, 1536), 1)
    offset = lax.broadcasted_iota(jnp.int32, (48, 1), 0)
    row = jnp.full((1, 1536), -1, jnp.int32)
    start = 0
    for b in range(BANDS):
        size = band_counts[b]
        inside = slot - 48 * b
        row = jnp.where((inside >= 0) & (inside < size), start + inside, row)
        slot_column[48 * b : 48 * b + 48, :] = jnp.where(offset < size, start + offset, -1)
        start = start + size
    slot_row[...] = row


def over_lanes(row, spread):
    return lax.dot_general(
        row,
        spread,
        (((1,), (1,)), ((), ())),
        precision=lax.Precision.HIGHEST,
        preferred_element_type=F32,
    )


def make_mixers(vert_modes, mode_depth, diffusion, balance, lane_scales, mixers):
    lane = lax.broadcasted_iota(jnp.int32, (128, 32), 0)
    level = lax.broadcasted_iota(jnp.int32, (128, 32), 1)
    spread = jnp.where((lane >> 5) * 8 + (lane & 7) == level, 1.0, 0.0)
    lane_scales[0:1, :] = over_lanes(diffusion[...], spread)
    lane_scales[1:2, :] = over_lanes(mode_depth[...], spread)
    spread = spread.astype(BF16)
    one = (lax.broadcasted_iota(jnp.int32, (128, 128), 0) >> 3) & 3
    two = (lax.broadcasted_iota(jnp.int32, (128, 128), 1) >> 3) & 3

    def widen(m, side):
        half = lax.dot_general(
            spread, m, (((1,), (side,)), ((), ())), preferred_element_type=F32
        ).astype(BF16)
        full = lax.dot_general(
            half, spread, (((1,), (1,)), ((), ())), preferred_element_type=F32
        )
        return jnp.where(one == two, full, 0.0).astype(BF16)

    for i, (m, side) in enumerate(((vert_modes, 1), (vert_modes, 0), (balance, 1))):
        high = m[...].astype(BF16)
        low = (m[...] - high.astype(F32)).astype(BF16)
        wide_high = widen(high, side)
        mixers[i, 0:128, 0:128] = wide_high
        mixers[i, 128:256, 0:128] = wide_high
        mixers[i, 0:128, 128:256] = widen(low, side)
        mixers[i, 128:256, 128:256] = jnp.zeros((128, 128), BF16)


PHASES = ((0, 2), (2, 2), (4, 3))


def place():
    lat, lev = lax.axis_index("lat"), lax.axis_index("lev")
    return lat, lev, lev * 32 + lat, lev * 32 + lax.rem(lat, 8) * 4 + lat // 8


def partners():
    lat, lev, _, _ = place()
    zs = [lax.rem(lat // 8 + i, 4) for i in range(4)]
    ys = [lax.rem(lat // 2 + i, 4) * 2 for i in range(4)]
    cores = [lax.rem(lat + i, 2) for i in range(2)]
    levs = [lax.rem(lev + i, 4) for i in range(4)]
    for k in range(1, 128):
        step = k * 37 % 128
        z, low = zs[step // 32], ys[step // 8 % 4] + cores[step % 2]
        x = levs[step // 2 % 4]
        yield (z * 8 + low, x), x * 32 + z * 8 + low, x * 32 + low * 4 + z


def greet_all():
    barrier = pltpu.get_barrier_semaphore()
    for to, _, _ in partners():
        pl.semaphore_signal(
            barrier, inc=1, device_id=to, device_id_type=pl.DeviceIdType.MESH
        )


def hear_all():
    pl.semaphore_wait(pltpu.get_barrier_semaphore(), 127)


def own_copy(phase, home, send, received, own_sem):
    _, _, plain, folded = place()
    first, count = PHASES[phase]
    tiles = pl.ds(first, count)
    source, target = (plain, folded) if home else (folded, plain)
    return pltpu.make_async_copy(send.at[source, tiles], received.at[target, tiles], own_sem)


def launch(phase, home, send, received, send_sem, recv_sem, own_sem):
    _, _, mine_plain, mine_folded = place()
    first, count = PHASES[phase]
    tiles = pl.ds(first, count)
    own_copy(phase, home, send, received, own_sem).start()
    for to, plain, folded in partners():
        pltpu.make_async_remote_copy(
            src_ref=send.at[plain if home else folded, tiles],
            dst_ref=received.at[mine_folded if home else mine_plain, tiles],
            send_sem=send_sem,
            recv_sem=recv_sem,
            device_id=to,
            device_id_type=pl.DeviceIdType.MESH,
        ).start()


def rest(phase, send, received, send_sem, recv_sem):
    lat, lev, _, _ = place()
    first, count = PHASES[phase]
    others = pl.ds(0, 127), pl.ds(first, count)
    return pltpu.make_async_remote_copy(
        src_ref=send.at[others],
        dst_ref=received.at[others],
        send_sem=send_sem,
        recv_sem=recv_sem,
        device_id=(lat, lev),
        device_id_type=pl.DeviceIdType.MESH,
    )


def arrive(phase, home, send, received, send_sem, recv_sem, own_sem):
    own_copy(phase, home, send, received, own_sem).wait()
    rest(phase, send, received, send_sem, recv_sem).wait_recv()


def wait_sent(phase, home, send, received, send_sem, recv_sem, own_sem):
    rest(phase, send, received, send_sem, recv_sem).wait_send()


def tiles_of(phase):
    first, count = PHASES[phase]
    return range(first, first + count)


def step_kernel(
    grid_hbm, legendre_hbm, pairs, pair_m, band_counts, gauss, vert_modes, mode_depth, diffusion,
    balance, out_hbm,
    grid, legendre, table, wave, b_cos, b_sin, a_cos, a_sin, y, chunks, turn,
    send, received, returned, wide, tall, fourier, spectral, updated, mixers, cross,
    weight, slot_row, slot_column, lane_scales,
    grid_sem, legendre_sem, out_sem, send_sem, recv_sem, own_sem,
):
    def field_of(ref, f):
        return ref.at[pl.ds(f * 384, 384)]

    for f in range(3):
        pltpu.make_async_copy(field_of(grid_hbm, f), field_of(grid, f), grid_sem.at[f]).start()
    pltpu.make_async_copy(legendre_hbm, legendre, legendre_sem).start()
    greet_all()
    chunks[27 * 64 :, :] = jnp.zeros((64, 1024), BF16)
    make_turn(turn)
    there = [
        (False, send, received, send_sem.at[i], recv_sem.at[i], own_sem.at[i]) for i in range(3)
    ]
    back = [
        (True, send, returned, send_sem.at[3 + i], recv_sem.at[3 + i], own_sem.at[3 + i])
        for i in range(3)
    ]
    row_weights(band_counts, gauss, weight)
    make_cross(cross)
    for p in range(3):
        make_table(p, pairs, table, wave, b_cos, b_sin, a_cos, a_sin)
        if p == 0:
            for f in range(3):
                pltpu.make_async_copy(
                    field_of(grid_hbm, f), field_of(grid, f), grid_sem.at[f]
                ).wait()
        analyse(p, grid, weight, table, y, wide, turn, chunks)

        def pack(t, carry):
            pack_chunks(t, chunks, cross, send)
            return carry

        lax.fori_loop(tiles_of(p)[0], tiles_of(p)[-1] + 1, pack, 0)
        if p == 0:
            hear_all()
        launch(p, *there[p])
    pltpu.make_async_copy(legendre_hbm, legendre, legendre_sem).wait()
    slot_latitudes(band_counts, slot_row, slot_column)
    make_mixers(vert_modes, mode_depth, diffusion, balance, lane_scales, mixers)
    lat, lev, _, _ = place()
    spread_legendre(0, legendre, slot_row, slot_column, wide, tall)
    for p in range(3):
        for phase in ((0, 1), (2,), ())[p]:
            arrive(phase, *there[phase])
            for t in tiles_of(phase):
                gather_tiles(t, received, cross, fourier)
        spectral_step(
            p, pair_m[3 * (4 * lat + lev) + p], lane_scales, mixers, wide, tall, fourier, spectral, updated
        )
        wait_sent(p, *there[p])
        for t in tiles_of(p):
            scatter_tiles(t, fourier, cross, send)
        launch(p, *back[p])
        if p == 0:


            def spread(other, carry):
                spread_legendre(other, legendre, slot_row, slot_column, wide, tall)
                return carry

            lax.fori_loop(1, 3, spread, 0)
    columns = wide.at[0:1152]
    done = 0
    for phase in range(3):
        arrive(phase, *back[phase])

        def unpack(t, carry):
            open_tiles(t, returned, cross, chunks)
            return carry

        lax.fori_loop(tiles_of(phase)[0], tiles_of(phase)[-1] + 1, unpack, 0)
        ready = min(4 * (tiles_of(phase)[-1] + 1), 27) // 3
        for unit in range(done, ready):
            arrange(unit // 3, unit % 3, chunks, y, columns)
        done = ready
        if phase == 1:

            def early(i, carry):
                synthesise(i, slice(0, 768), 0, 1024, columns, table, grid, False)
                synthesise(i, slice(768, 1152), 0, 512, columns, table, grid, False)
                return carry

            lax.fori_loop(0, POINTS // 256, early, 0)

    def part_of(ref, i):
        return ref.at[:, pl.ds(pl.multiple_of(i * 256, 256), 256)]

    def points(i, carry):
        synthesise(i, slice(0, 768), 1024, 1536, columns, table, grid, True)
        synthesise(i, slice(768, 1152), 512, 1536, columns, table, grid, True)
        pltpu.make_async_copy(part_of(grid, i), part_of(out_hbm, i), out_sem).start()
        return carry

    lax.fori_loop(0, POINTS // 256, points, 0)
    pltpu.make_async_copy(grid, out_hbm, out_sem).wait()
    for phase in range(3):
        wait_sent(phase, *back[phase])


def step(*inputs):
    vmem = pl.BlockSpec(memory_space=pltpu.VMEM)
    smem = pl.BlockSpec(memory_space=pltpu.SMEM)
    hbm = pl.BlockSpec(memory_space=pl.ANY)
    block = (128, 7, 16, 128)
    scratch = [
        ((1152, POINTS), BF16),
        ((3, WIDTH + 1, NLAT), BF16),
        ((POINTS, 1536), BF16),
        ((1, 512), F32),
        ((128, 512), F32),
        ((128, 512), F32),
        ((24, 512), F32),
        ((24, 512), F32),
        ((4, 384, 128), F32),
        ((28 * 64, 1024), BF16),
        ((1024, 1024), BF16),
        (block, BF16),
        (block, BF16),
        (block, BF16),
        ((3 * ROWS, 1536), BF16),
        ((3, 1536, DEPTH), BF16),
        ((3, 32, 3, 16, 384), BF16),
        ((ROWS, 384), F32),
        ((DEPTH, 384), BF16),
        ((3, 256, 256), BF16),
        ((512, 512), BF16),
        ((384, 128), F32),
        ((1, 1536), jnp.int32),
        ((1536, 1), jnp.int32),
        ((2, 128), F32),
    ]
    dma = pltpu.SemaphoreType.DMA
    return pl.pallas_call(
        step_kernel,
        out_shape=jax.ShapeDtypeStruct((1152, POINTS), BF16),
        in_specs=[hbm, hbm, vmem, smem, smem, smem] + [vmem] * 4,
        out_specs=hbm,
        scratch_shapes=[pltpu.VMEM(s, d) for s, d in scratch]
        + [dma((3,)), dma, dma, dma((6,)), dma((6,)), dma((6,))],
        compiler_params=pltpu.CompilerParams(
            vmem_limit_bytes=67043328, collective_id=0, has_side_effects=True
        ),
    )(*inputs)


def shards(
    grid,
    legendre,
    gauss_weights,
    band_counts,
    pair_m,
    vert_modes,
    mode_depth,
    diffusion,
    pressure_balance_matrix,
):
    fields, lat_cap, lev_dev, points = grid.shape
    out = step(
        grid.reshape(fields * lat_cap * lev_dev, points),
        legendre,
        pair_m,
        pair_m,
        band_counts,
        gauss_weights,
        vert_modes,
        mode_depth.reshape(1, 32),
        diffusion.reshape(1, 32),
        pressure_balance_matrix,
    )
    return out.reshape(fields, lat_cap, lev_dev, points)


def solution(mesh):
    placed = (
        P(None, "lat", "lev", None),
        P(("lat", "lev"), None, None),
        P(),
        P(),
        P(),
        P(),
        P(),
        P(),
        P(),
    )
    return jax.shard_map(
        shards, mesh=mesh, in_specs=placed, out_specs=P(None, "lat", "lev", None), check_vma=False
    )
```

```python
import math

import jax
import jax.numpy as jnp
from jax import lax
from jax.experimental import pallas as pl
from jax.experimental.pallas import tpu as pltpu
from jax.sharding import PartitionSpec as P

WIDTH = 768
NLAT = 1280
POINTS = 2816
ROWS = 784
DEPTH = 896
BANDS = 32
F32, BF16 = jnp.float32, jnp.bfloat16

WINDOWS = ((0, 256), (0, 512), (256, 512), (512, 512), (768, 512), (1024, 256))


def swap(a, b, bit, low):
    return (
        jnp.where(low, a, pltpu.roll(b, bit, 1)),
        jnp.where(low, pltpu.roll(a, 128 - bit, 1), b),
    )


def exchange_bits(arrays, base, lane):
    arrays = list(arrays)
    step = 1
    while step < len(arrays):
        bit = base * step
        low = (lane & bit) == 0
        for i in range(len(arrays)):
            if not i & step:
                arrays[i], arrays[i | step] = swap(arrays[i], arrays[i | step], bit, low)
        step *= 2
    return arrays


def each(total, together, load, base, store):
    lane = lanes_of()

    def body(i, carry):
        groups = [load(i * together + u) for u in range(together)]
        groups = [exchange_bits(parts, base, lane) for parts in groups]
        for u, parts in enumerate(groups):
            store(i * together + u, parts)
        return carry

    lax.fori_loop(0, total // together, body, 0)


def lanes_of(rows=16):
    return lax.broadcasted_iota(jnp.int32, (rows, 128), 1)


def cos_sin(value, turn):
    quarter = POINTS // 4
    index = jnp.floor(value * (1.0 / quarter) + 0.5)
    angle = (value - index * quarter) * (2.0 * math.pi / POINTS)
    sq = angle * angle
    c = 1.0 + sq * (-0.5 + sq * (1 / 24 + sq * (-1 / 720 + sq * (1 / 40320))))
    s = angle * (1.0 + sq * (-1 / 6 + sq * (1 / 120 + sq * (-1 / 5040))))
    index = (index.astype(jnp.int32) + turn) & 3
    odd = (index & 1) == 1
    cos = jnp.where(odd, s, c)
    sin = jnp.where(odd, c, s)
    cos = jnp.where((index == 1) | (index == 2), -cos, cos)
    sin = jnp.where(index >= 2, -sin, sin)
    return cos, sin


def make_table(p, pairs, table, wave, b_cos, b_sin, a_cos, a_sin):
    lane = lax.broadcasted_iota(jnp.int32, (128, 128), 1)
    device = lax.broadcasted_iota(jnp.int32, (128, 128), 0)
    lane384 = lax.broadcasted_iota(jnp.int32, (128, 384), 1)
    device384 = lax.broadcasted_iota(jnp.int32, (128, 384), 0)
    pair = pairs[...].reshape(1, 384).astype(F32)
    lower = jnp.where(lane384 == 3 * device384 + p, pair, 0.0)
    lower = jnp.sum(lower, axis=1, keepdims=True)
    upper = (lanes_of(1) & 16) != 0
    for tile in range(4):
        chosen = device == 32 * tile + 4 * (lane & 7) + (lane >> 5)
        low = jnp.sum(jnp.where(chosen, lower, 0.0), axis=0, keepdims=True)
        wave[:, tile * 128 : tile * 128 + 128] = jnp.where(upper, WIDTH - 1 - low, low)
    w = wave[...]
    row = lax.broadcasted_iota(jnp.int32, (128, 512), 0).astype(F32)
    b_cos[...], b_sin[...] = cos_sin(row * w, 0)
    row = lax.broadcasted_iota(jnp.int32, (24, 512), 0).astype(F32)
    part = (lax.broadcasted_iota(jnp.int32, (24, 512), 1) >> 3) & 1
    a_cos[...], a_sin[...] = cos_sin(row * (128.0 * w), part)

    def fill(a, carry):
        values = a_cos[pl.ds(a, 1), :] * b_cos[...] - a_sin[pl.ds(a, 1), :] * b_sin[...]
        rows = pl.ds(pl.multiple_of(a * 128, 128), 128)
        table[rows, p * 512 : p * 512 + 512] = values.astype(BF16)
        return carry

    lax.fori_loop(0, POINTS // 128, fill, 0)


def analyse(p, grid, weight, table, y, stage, turn, chunks):
    def field(f, carry):
        base = pl.multiple_of(f * 384, 384)
        values = jnp.dot(
            grid[pl.ds(base, 384), :],
            table[:, p * 512 : p * 512 + 512],
            preferred_element_type=F32,
        )
        for tile in range(4):
            y[tile] = values[:, tile * 128 : tile * 128 + 128] * weight[...]

        for third in range(3):
            for tile in range(4):
                at = pl.multiple_of(f * 192 + (4 * third + tile) * 16, 16)
                for l in range(8):
                    stage[pl.ds(at, 16), l * 128 : l * 128 + 128] = y[
                        tile, pl.ds(third * 128 + l, 16, stride=8), :
                    ].astype(BF16)
        return carry

    lax.fori_loop(0, 3, field, 0)
    chunks[p * 576 : p * 576 + 576, :] = jnp.dot(
        stage[0:576, 0:1024], turn[...], preferred_element_type=F32
    ).astype(BF16)


def crossed(parts, cross):
    whole = jnp.concatenate([part.reshape(512, 128) for part in parts], axis=1)
    out = jnp.dot(whole, cross[...], preferred_element_type=F32).astype(BF16)
    return [out[:, i * 128 : i * 128 + 128].reshape(32, 16, 128) for i in range(4)]


def fours(i):
    return pl.ds(32 * i, 32)


def pack_chunks(t, chunks, cross, send):
    parts = []
    for g in range(4):
        rows = chunks[pl.ds(pl.multiple_of(t * 256 + g * 64, 64), 64), :]
        parts.append(
            jnp.concatenate([rows[:, e * 128 : e * 128 + 128] for e in range(8)], axis=0)
        )
    for x, out in enumerate(crossed(parts, cross)):
        send[fours(x), t] = out


def make_turn(turn):
    source = lax.broadcasted_iota(jnp.int32, (1024, 128), 0)
    target = lax.broadcasted_iota(jnp.int32, (1024, 128), 1)
    for e in range(8):
        from_lane = (target & 7) * 128 + (target >> 3) * 8 + e
        turn[:, e * 128 : e * 128 + 128] = jnp.where(source == from_lane, 1.0, 0.0).astype(BF16)


def make_cross(cross):
    source = lax.broadcasted_iota(jnp.int32, (512, 512), 0)
    target = lax.broadcasted_iota(jnp.int32, (512, 512), 1)
    from_lane = ((source >> 5) & 3) * 128 + (source >> 7) * 32 + (source & 31)
    cross[...] = jnp.where(from_lane == target, 1.0, 0.0).astype(BF16)


def spread_legendre(p, legendre, slot_row, slot_column, wide, tall):
    base = p * ROWS if isinstance(p, int) else pl.multiple_of(p * ROWS, 16)
    wide[pl.ds(base + 768, 16), :] = jnp.zeros((16, 1536), BF16)
    tall[p, :, 768:DEPTH] = jnp.zeros((1536, 128), BF16)
    for tile, (low, size) in enumerate(WINDOWS):
        at = slice(tile * 256, tile * 256 + 256)
        part = legendre[p, :, low : low + size]
        row = lax.broadcasted_iota(jnp.int32, (size, 256), 0) + low
        pick = jnp.where(row == slot_row[:, at], 1.0, 0.0).astype(BF16)
        wide[pl.ds(base, WIDTH + 1), at] = jnp.dot(
            part, pick, preferred_element_type=F32
        ).astype(BF16)
        row = lax.broadcasted_iota(jnp.int32, (256, size), 1) + low
        pick = jnp.where(row == slot_column[at, :], 1.0, 0.0).astype(BF16)
        tall[p, at, 0 : WIDTH + 1] = lax.dot_general(
            pick, part, (((1,), (1,)), ((), ())), preferred_element_type=F32
        ).astype(BF16)


def gather_tiles(t, received, cross, fourier):
    for g, out in enumerate(crossed([received[fours(v), t] for v in range(4)], cross)):
        q = 4 * t + g
        if q < 27:
            f, third = q % 9 // 3, q % 3
            fourier[q // 9, :, third, :, f * 128 : f * 128 + 128] = out


def mixed(values, mixer):
    high = values.astype(BF16)
    low = (values - high.astype(F32)).astype(BF16)
    out = jnp.dot(
        jnp.concatenate([high, low], axis=1), mixer, preferred_element_type=F32
    )
    return out[:, 0:128] + out[:, 128:256]


def spectral_step(p, wave, lane_scales, mixers, wide, tall, fourier, spectral, updated):
    spectral[...] = jnp.dot(
        wide[p * ROWS : p * ROWS + ROWS, :],
        fourier[p].reshape(1536, 384),
        preferred_element_type=F32,
    )
    updated[ROWS:DEPTH, :] = jnp.zeros((DEPTH - ROWS, 384), BF16)
    for at, size in ((0, 400), (400, 384)):
        k = lax.broadcasted_iota(jnp.int32, (size, 128), 0) + at
        own = k < WIDTH - wave
        degree = jnp.where(own, wave + k, k - 1)
        ratio = (degree * (degree + 1)).astype(F32) * (1.0 / float(WIDTH * (WIDTH - 1)))
        keep = (own != ((lanes_of(size) & 16) != 0)) & (k <= WIDTH)
        rows = slice(at, at + size)
        first = spectral[rows, 0:128] / (1.0 + lane_scales[0:1, :] * ratio * ratio)
        modes = mixed(spectral[rows, 128:256], mixers[0])
        modes = modes / (1.0 + lane_scales[1:2, :] * ratio)
        second = mixed(modes, mixers[1])
        third = spectral[rows, 256:384] - mixed(second, mixers[2])
        for f, values in enumerate((first, second, third)):
            updated[rows, f * 128 : f * 128 + 128] = jnp.where(keep, values, 0.0).astype(BF16)
    double = (lax.broadcasted_iota(jnp.int32, (1, 384), 1) & 16 != 0) | (wave > 0)
    factor = jnp.where(double, 2.0, 1.0)

    def rows_of(i, carry):
        at = pl.multiple_of(i * 384, 384)
        values = jnp.dot(tall[p, pl.ds(at, 384), :], updated[...], preferred_element_type=F32)
        out = (values * factor).astype(BF16)
        fourier[p, pl.ds(pl.multiple_of(i * 8, 8), 8)] = out.reshape(8, 3, 16, 384)
        return carry

    lax.fori_loop(0, 4, rows_of, 0)


def scatter_tiles(t, synthesis, cross, send):
    parts = []
    for q in range(4 * t, 4 * t + 4):
        q = min(q, 26)
        f, third = q % 9 // 3, q % 3
        parts.append(synthesis[q // 9, :, third, :, f * 128 : f * 128 + 128])
    for v, out in enumerate(crossed(parts, cross)):
        send[fours(v), t] = out


def open_tiles(t, received, cross, chunks):
    for g, out in enumerate(crossed([received[fours(x), t] for x in range(4)], cross)):
        rows = pl.ds(pl.multiple_of(t * 256 + g * 64, 64), 64)
        out = out.reshape(512, 128)
        for e in range(8):
            chunks[rows, e * 128 : e * 128 + 128] = out[e * 64 : e * 64 + 64]


def arrange(p, f, chunks, y, columns):
    def load(n):
        third, tile = n // 4, lax.rem(n, 4)
        at = pl.multiple_of((9 * p + 3 * f + third) * 64 + tile * 16, 16)
        return [chunks[pl.ds(at, 16), e * 128 : e * 128 + 128] for e in range(8)]

    def store(n, parts):
        third, tile = n // 4, lax.rem(n, 4)
        for l, values in enumerate(parts):
            y[tile, pl.ds(third * 128 + l, 16, stride=8), :] = values.astype(F32)

    each(12, 4, load, 1, store)
    for tile in range(4):
        at = p * 512 + tile * 128
        columns[f * 384 : f * 384 + 384, at : at + 128] = y[tile].astype(BF16)


def synthesise(i, rows, low, high, columns, table, out, add):
    at = pl.ds(pl.multiple_of(i * 256, 256), 256)
    values = lax.dot_general(
        columns[rows, low:high],
        table[at, low:high],
        (((1,), (1,)), ((), ())),
        preferred_element_type=F32,
    )
    if add:
        values = values + out[rows, at].astype(F32)
    out[rows, at] = values.astype(BF16)


def row_weights(band_counts, gauss, weight):
    lat = lax.axis_index("lat")
    start, count = 0, 0
    for b in range(BANDS):
        size = band_counts[b]
        start = start + jnp.where(b < lat, size, 0)
        count = count + jnp.where(b == lat, size, 0)
    for r in range(48):
        value = gauss[jnp.minimum(start + r, NLAT - 1)] * (1.0 / POINTS)
        value = jnp.where(r < count, value, 0.0)
        weight[8 * r : 8 * r + 8, :] = jnp.broadcast_to(value, (8, 128))


def slot_latitudes(band_counts, slot_row, slot_column):
    slot = lax.broadcasted_iota(jnp.int32, (1, 1536), 1)
    offset = lax.broadcasted_iota(jnp.int32, (48, 1), 0)
    row = jnp.full((1, 1536), -1, jnp.int32)
    start = 0
    for b in range(BANDS):
        size = band_counts[b]
        inside = slot - 48 * b
        row = jnp.where((inside >= 0) & (inside < size), start + inside, row)
        slot_column[48 * b : 48 * b + 48, :] = jnp.where(offset < size, start + offset, -1)
        start = start + size
    slot_row[...] = row


def over_lanes(row, spread):
    return lax.dot_general(
        row,
        spread,
        (((1,), (1,)), ((), ())),
        precision=lax.Precision.HIGHEST,
        preferred_element_type=F32,
    )


def make_mixers(vert_modes, mode_depth, diffusion, balance, lane_scales, mixers):
    lane = lax.broadcasted_iota(jnp.int32, (128, 32), 0)
    level = lax.broadcasted_iota(jnp.int32, (128, 32), 1)
    spread = jnp.where((lane >> 5) * 8 + (lane & 7) == level, 1.0, 0.0)
    lane_scales[0:1, :] = over_lanes(diffusion[...], spread)
    lane_scales[1:2, :] = over_lanes(mode_depth[...], spread)
    spread = spread.astype(BF16)
    one = (lax.broadcasted_iota(jnp.int32, (128, 128), 0) >> 3) & 3
    two = (lax.broadcasted_iota(jnp.int32, (128, 128), 1) >> 3) & 3

    def widen(m, side):
        half = lax.dot_general(
            spread, m, (((1,), (side,)), ((), ())), preferred_element_type=F32
        ).astype(BF16)
        full = lax.dot_general(
            half, spread, (((1,), (1,)), ((), ())), preferred_element_type=F32
        )
        return jnp.where(one == two, full, 0.0).astype(BF16)

    for i, (m, side) in enumerate(((vert_modes, 1), (vert_modes, 0), (balance, 1))):
        high = m[...].astype(BF16)
        low = (m[...] - high.astype(F32)).astype(BF16)
        wide_high = widen(high, side)
        mixers[i, 0:128, 0:128] = wide_high
        mixers[i, 128:256, 0:128] = wide_high
        mixers[i, 0:128, 128:256] = widen(low, side)
        mixers[i, 128:256, 128:256] = jnp.zeros((128, 128), BF16)


PHASES = ((0, 2), (2, 2), (4, 3))
RETURNS = ((0, 2), (2, 2), (4, 2), (6, 1))


def place():
    lat, lev = lax.axis_index("lat"), lax.axis_index("lev")
    return lat, lev, lev * 32 + lat, lev * 32 + lax.rem(lat, 8) * 4 + lat // 8


def partners():
    lat, lev, _, _ = place()
    zs = [lax.rem(lat // 8 + i, 4) for i in range(4)]
    ys = [lax.rem(lat // 2 + i, 4) * 2 for i in range(4)]
    cores = [lax.rem(lat + i, 2) for i in range(2)]
    levs = [lax.rem(lev + i, 4) for i in range(4)]
    for k in range(1, 128):
        step = k * 37 % 128
        z, low = zs[step // 32], ys[step // 8 % 4] + cores[step % 2]
        x = levs[step // 2 % 4]
        yield (z * 8 + low, x), x * 32 + z * 8 + low, x * 32 + low * 4 + z


def greet_all():
    barrier = pltpu.get_barrier_semaphore()
    for to, _, _ in partners():
        pl.semaphore_signal(
            barrier, inc=1, device_id=to, device_id_type=pl.DeviceIdType.MESH
        )


def hear_all():
    pl.semaphore_wait(pltpu.get_barrier_semaphore(), 127)


def own_copy(phase, home, send, received, own_sem):
    _, _, plain, folded = place()
    tiles = pl.ds(*phase)
    source, target = (plain, folded) if home else (folded, plain)
    return pltpu.make_async_copy(send.at[source, tiles], received.at[target, tiles], own_sem)


def launch(phase, home, send, received, send_sem, recv_sem, own_sem):
    _, _, mine_plain, mine_folded = place()
    tiles = pl.ds(*phase)
    own_copy(phase, home, send, received, own_sem).start()
    for to, plain, folded in partners():
        pltpu.make_async_remote_copy(
            src_ref=send.at[plain if home else folded, tiles],
            dst_ref=received.at[mine_folded if home else mine_plain, tiles],
            send_sem=send_sem,
            recv_sem=recv_sem,
            device_id=to,
            device_id_type=pl.DeviceIdType.MESH,
        ).start()


def rest(phase, send, received, send_sem, recv_sem):
    lat, lev, _, _ = place()
    others = pl.ds(0, 127), pl.ds(*phase)
    return pltpu.make_async_remote_copy(
        src_ref=send.at[others],
        dst_ref=received.at[others],
        send_sem=send_sem,
        recv_sem=recv_sem,
        device_id=(lat, lev),
        device_id_type=pl.DeviceIdType.MESH,
    )


def arrive(phase, home, send, received, send_sem, recv_sem, own_sem):
    own_copy(phase, home, send, received, own_sem).wait()
    rest(phase, send, received, send_sem, recv_sem).wait_recv()


def wait_sent(phase, home, send, received, send_sem, recv_sem, own_sem):
    rest(phase, send, received, send_sem, recv_sem).wait_send()


def tiles_of(phase):
    return range(phase[0], phase[0] + phase[1])


def step_kernel(
    grid_hbm, legendre_hbm, pairs, pair_m, band_counts, gauss, vert_modes, mode_depth, diffusion,
    balance, out_hbm,
    grid, legendre, table, wave, b_cos, b_sin, a_cos, a_sin, y, chunks, turn,
    send, received, returned, wide, tall, fourier, spectral, updated, mixers, cross,
    weight, slot_row, slot_column, lane_scales,
    grid_sem, legendre_sem, out_sem, send_sem, recv_sem, own_sem,
):
    def field_of(ref, f):
        return ref.at[pl.ds(f * 384, 384)]

    for f in range(3):
        pltpu.make_async_copy(field_of(grid_hbm, f), field_of(grid, f), grid_sem.at[f]).start()
    pltpu.make_async_copy(legendre_hbm, legendre, legendre_sem).start()
    greet_all()
    chunks[27 * 64 :, :] = jnp.zeros((64, 1024), BF16)
    make_turn(turn)
    there = [
        (PHASES[i], False, send, received, send_sem.at[i], recv_sem.at[i], own_sem.at[i])
        for i in range(3)
    ]
    back = [
        (RETURNS[i], True, send, returned, send_sem.at[3 + i], recv_sem.at[3 + i], own_sem.at[3 + i])
        for i in range(4)
    ]
    row_weights(band_counts, gauss, weight)
    make_cross(cross)
    for p in range(3):
        make_table(p, pairs, table, wave, b_cos, b_sin, a_cos, a_sin)
        if p == 0:
            for f in range(3):
                pltpu.make_async_copy(
                    field_of(grid_hbm, f), field_of(grid, f), grid_sem.at[f]
                ).wait()
        analyse(p, grid, weight, table, y, wide, turn, chunks)

        def pack(t, carry):
            pack_chunks(t, chunks, cross, send)
            return carry

        lax.fori_loop(tiles_of(PHASES[p])[0], tiles_of(PHASES[p])[-1] + 1, pack, 0)
        if p == 0:
            hear_all()
        launch(*there[p])
    pltpu.make_async_copy(legendre_hbm, legendre, legendre_sem).wait()
    slot_latitudes(band_counts, slot_row, slot_column)
    make_mixers(vert_modes, mode_depth, diffusion, balance, lane_scales, mixers)
    lat, lev, _, _ = place()
    spread_legendre(0, legendre, slot_row, slot_column, wide, tall)
    for p in range(3):
        for phase in ((0, 1), (2,), ())[p]:
            arrive(*there[phase])
            for t in tiles_of(PHASES[phase]):
                gather_tiles(t, received, cross, fourier)
        spectral_step(
            p, pair_m[3 * (4 * lat + lev) + p], lane_scales, mixers, wide, tall, fourier, spectral, updated
        )
        wait_sent(*there[p])
        for i in ((0,), (1,), (2, 3))[p]:
            for t in tiles_of(RETURNS[i]):
                scatter_tiles(t, fourier, cross, send)
            launch(*back[i])
        if p == 0:


            def spread(other, carry):
                spread_legendre(other, legendre, slot_row, slot_column, wide, tall)
                return carry

            lax.fori_loop(1, 3, spread, 0)
    columns = wide.at[0:1152]
    upper, lower = slice(0, 768), slice(768, 1152)

    def each_part(work):
        def body(i, carry):
            work(i)
            return carry

        lax.fori_loop(0, POINTS // 256, body, 0)

    def emit(i, rows, sem):
        at = rows, pl.ds(pl.multiple_of(i * 256, 256), 256)
        pltpu.make_async_copy(grid.at[at], out_hbm.at[at], sem).start()

    def early(i):
        synthesise(i, upper, 0, 1024, columns, table, grid, False)
        synthesise(i, lower, 0, 512, columns, table, grid, False)

    def middle(i):
        synthesise(i, upper, 1024, 1536, columns, table, grid, True)
        emit(i, upper, out_sem.at[0])
        synthesise(i, lower, 512, 1024, columns, table, grid, True)

    def late(i):
        synthesise(i, lower, 1024, 1536, columns, table, grid, True)
        emit(i, lower, out_sem.at[1])

    done = 0
    for i in range(4):
        arrive(*back[i])

        def unpack(t, carry):
            open_tiles(t, returned, cross, chunks)
            return carry

        tiles = tiles_of(RETURNS[i])
        lax.fori_loop(tiles[0], tiles[-1] + 1, unpack, 0)
        ready = min(4 * (tiles[-1] + 1), 27) // 3
        for unit in range(done, ready):
            arrange(unit // 3, unit % 3, chunks, y, columns)
        done = ready
        if i:
            each_part((None, early, middle, late)[i])
    for rows, sem in ((upper, out_sem.at[0]), (lower, out_sem.at[1])):
        pltpu.make_async_copy(grid.at[rows], out_hbm.at[rows], sem).wait()
    for i in range(4):
        wait_sent(*back[i])


def step(*inputs):
    vmem = pl.BlockSpec(memory_space=pltpu.VMEM)
    smem = pl.BlockSpec(memory_space=pltpu.SMEM)
    hbm = pl.BlockSpec(memory_space=pl.ANY)
    block = (128, 7, 16, 128)
    scratch = [
        ((1152, POINTS), BF16),
        ((3, WIDTH + 1, NLAT), BF16),
        ((POINTS, 1536), BF16),
        ((1, 512), F32),
        ((128, 512), F32),
        ((128, 512), F32),
        ((24, 512), F32),
        ((24, 512), F32),
        ((4, 384, 128), F32),
        ((28 * 64, 1024), BF16),
        ((1024, 1024), BF16),
        (block, BF16),
        (block, BF16),
        (block, BF16),
        ((3 * ROWS, 1536), BF16),
        ((3, 1536, DEPTH), BF16),
        ((3, 32, 3, 16, 384), BF16),
        ((ROWS, 384), F32),
        ((DEPTH, 384), BF16),
        ((3, 256, 256), BF16),
        ((512, 512), BF16),
        ((384, 128), F32),
        ((1, 1536), jnp.int32),
        ((1536, 1), jnp.int32),
        ((2, 128), F32),
    ]
    dma = pltpu.SemaphoreType.DMA
    return pl.pallas_call(
        step_kernel,
        out_shape=jax.ShapeDtypeStruct((1152, POINTS), BF16),
        in_specs=[hbm, hbm, vmem, smem, smem, smem] + [vmem] * 4,
        out_specs=hbm,
        scratch_shapes=[pltpu.VMEM(s, d) for s, d in scratch]
        + [dma((3,)), dma, dma((2,)), dma((7,)), dma((7,)), dma((7,))],
        compiler_params=pltpu.CompilerParams(
            vmem_limit_bytes=67043328, collective_id=0, has_side_effects=True
        ),
    )(*inputs)


def shards(
    grid,
    legendre,
    gauss_weights,
    band_counts,
    pair_m,
    vert_modes,
    mode_depth,
    diffusion,
    pressure_balance_matrix,
):
    fields, lat_cap, lev_dev, points = grid.shape
    out = step(
        grid.reshape(fields * lat_cap * lev_dev, points),
        legendre,
        pair_m,
        pair_m,
        band_counts,
        gauss_weights,
        vert_modes,
        mode_depth.reshape(1, 32),
        diffusion.reshape(1, 32),
        pressure_balance_matrix,
    )
    return out.reshape(fields, lat_cap, lev_dev, points)


def solution(mesh):
    placed = (
        P(None, "lat", "lev", None),
        P(("lat", "lev"), None, None),
        P(),
        P(),
        P(),
        P(),
        P(),
        P(),
        P(),
    )
    return jax.shard_map(
        shards, mesh=mesh, in_specs=placed, out_specs=P(None, "lat", "lev", None), check_vma=False
    )
```
